32 devices in a mesh: dp: 8 (over z, x), tensor: 4 (over y, core).
Axes of the slice: x: 2, y: 2, z: 4, core: 2. Of those that a mesh axis runs over, the one named last changes fastest.
Arguments:
- layer_input: bfloat16 [16, 512, 2048], P('dp'), may hold values from -6 to 6
- segments: int32 [16, 512], P('dp'), may hold values from 0 to 3, never falling along the last dimension, each value on 1 to 256 neighbouring positions
- query_weight: bfloat16 [2048, 2048], P('dp', 'tensor'), may hold values from -0.125 to 0.125
- key_matrix: bfloat16 [2048, 1024], P('dp', 'tensor'), may hold values from -0.125 to 0.125
- value_matrix: bfloat16 [2048, 1024], P('dp', 'tensor'), may hold values from -0.125 to 0.125
- gate_weight: bfloat16 [2048, 2048], P('dp', 'tensor'), may hold values from -0.125 to 0.125
- out_weight: bfloat16 [2048, 2048], P('tensor', 'dp'), may hold values from -1 to 1
- ffn_gate_weight: bfloat16 [2048, 6144], P('dp', 'tensor'), may hold values from -0.125 to 0.125
- ffn_up_weight: bfloat16 [2048, 6144], P('dp', 'tensor'), may hold values from -0.125 to 0.125
- ffn_down_weight: bfloat16 [6144, 2048], P('tensor', 'dp'), may hold values from -0.109375 to 0.109375
- attn_gain: float32 [2048], replicated, may hold values from 0.5 to 1.5
- ffn_gain: float32 [2048], replicated, may hold values from 0.5 to 1.5
- query_gain: float32 [128], replicated, may hold values from 0.1 to 1.9
- key_norm_gain: float32 [128], replicated, may hold values from 0.1 to 1.9
- cotangent: bfloat16 [16, 512, 2048], P('dp'), may hold values from -6 to 6
Outputs:
- output: bfloat16 [16, 512, 2048], P('dp')
- input_grad: float32 [16, 512, 2048], P('dp')
- grad_query_weight: float32 [2048, 2048], P('dp', 'tensor')
- grad_key_weight: float32 [2048, 1024], P('dp', 'tensor')
- grad_value_weight: float32 [2048, 1024], P('dp', 'tensor')
- grad_gate_weight: float32 [2048, 2048], P('dp', 'tensor')
- grad_out_weight: float32 [2048, 2048], P('tensor', 'dp')
- grad_ffn_gate_weight: float32 [2048, 6144], P('dp', 'tensor')
- grad_ffn_up_weight: float32 [2048, 6144], P('dp', 'tensor')
- grad_ffn_down_weight: float32 [6144, 2048], P('tensor', 'dp')
- grad_attn_gain: float32 [2048], replicated
- grad_ffn_gain: float32 [2048], replicated
- grad_query_gain: float32 [128], replicated
- grad_key_gain: float32 [128], replicated
The draws below stay inside these ranges and needn't reach their ends.
Inputs may be any that keep to these rules, and one draw needn't show every extreme that they name: `segments`: segment numbers never fall along a sequence; each document holds 1 to 256 tokens and some document holds exactly 256.
All inputs are finite; a program needn't handle non-finite values.
Results may differ from the reference program's by a relative error of at most 0.02.
Values may be sent and summed in bfloat16 or wider, within the bound.
No kernel may reach another device: no remote copies, remote signals or barrier semaphores. Data moves between devices by JAX's collectives and lax.ppermute only.
A program may use at most 256 MiB of HBM per device.

```python
import math
import jax
import jax.numpy as jnp
import numpy as np
from jax import lax

MODEL_WIDTH = 2048
QUERY_HEADS = 16
KEY_VALUE_HEADS = 8
HEAD_WIDTH = 128
FF = 6144
SEQ = 512
SEQS = 16


def spiked(values, key, source, target, blocks, factor):
    owner, partner = [(jnp.arange(values.shape[dim]) // (values.shape[dim] // blocks)).reshape([-1 if axis == dim else 1 for axis in range(values.ndim)]) for dim in (source, target)]
    chosen = jax.random.permutation(key, blocks)[partner]
    strong = (owner == chosen) | (owner == (partner + blocks // 2) % blocks)
    return jnp.where(strong, factor * values, values)


def block_scale(stream_key, extent, pieces, smallest, high):
    level, own = 1.0, jax.random.fold_in(stream_key, 6)
    for dim, parts in pieces:
        steps = jnp.exp(jax.random.uniform(jax.random.fold_in(own, dim), (parts,), jnp.float32, smallest / len(pieces), high / len(pieces)))
        level = level * jnp.repeat(steps, extent[dim] // parts).reshape([-1 if axis == dim else 1 for axis in range(len(extent))])
    return level


def split_up(count, total, most, lean):
    loads = [(1 << 20) // math.isqrt(standing ** lean) + 1 for standing in range(2, count + 1)]
    spare, holding = total - most - (count - 1), [1] * (count - 1)
    while spare > 0:
        free = [i for i in range(count - 1) if holding[i] < most]
        mass, budget = sum([loads[i] for i in free]), spare
        for i in free:
            addition = min(most - holding[i], max(1, budget * loads[i] // mass), spare)
            holding[i] = holding[i] + addition
            spare = spare - addition
    return np.array([most] + holding)


def uneven_parts(own_key, amount, total, most, lean):
    if amount == 2:
        one = jax.random.randint(own_key, (), max(1, total - most), min(most, total - 1) + 1)
        return jnp.stack([one, total - one])
    sizes = jnp.asarray(split_up(amount, total, most, lean), jnp.int32)
    twos = (amount - 1) // 2
    giver, receiver = sizes[1:1 + 2 * twos:2], sizes[2:2 + 2 * twos:2]
    slack = jnp.minimum(giver - 1, most - receiver)
    shifted = jax.random.randint(jax.random.fold_in(own_key, 1), (twos,), 0, 1 << 20) % (slack + 1)
    sizes = sizes.at[1:1 + 2 * twos:2].set(giver - shifted).at[2:2 + 2 * twos:2].set(receiver + shifted)
    return sizes[jax.random.permutation(jax.random.fold_in(own_key, 2), amount)]


def normal_values(rng, extent, deviation, bound, shards=(), kind=jnp.bfloat16):
    values = jax.random.normal(rng, extent, jnp.float32) * deviation
    if len(shards) > 0:
        values = block_scale(rng, extent, shards, -0.22, 0.18) * values
    return jnp.clip(values, min=-bound, max=bound).astype(kind)


def heavy_noise(rng, shape, spread, reach, shards, heavy, kind=jnp.bfloat16):
    array = spread * jax.random.normal(rng, shape, jnp.float32)
    if shards:
        array = array * block_scale(rng, shape, shards, -0.22, 0.18)
    return jnp.clip(spiked(array, jax.random.fold_in(rng, 3), *heavy), -reach, reach).astype(kind)


def setup_inputs(seed: int = 0) -> dict:
    key_list = jax.random.split(jax.random.key(seed), 16)
    return {
        "layer_input": heavy_noise(key_list[0], (SEQS, SEQ, MODEL_WIDTH), 1.0, 6.0, ((0, 8),), (0, 2, 8, 2.0)),
        "segments": jax.vmap(lambda own: jnp.searchsorted(jnp.cumsum(uneven_parts(own, 4, SEQ, SEQ // 2, 2)), jnp.arange(SEQ), side="right"))(jax.random.split(key_list[1], SEQS)).reshape((SEQS, SEQ)).astype(jnp.int32),
        "query_weight": normal_values(key_list[2], (MODEL_WIDTH, QUERY_HEADS * HEAD_WIDTH), MODEL_WIDTH ** -0.5, 0.125, ((0, 8), (1, 4))),
        "key_matrix": normal_values(key_list[3], (MODEL_WIDTH, KEY_VALUE_HEADS * HEAD_WIDTH), MODEL_WIDTH ** -0.5, 0.125, ((0, 8), (1, 4))),
        "value_matrix": normal_values(key_list[4], (MODEL_WIDTH, KEY_VALUE_HEADS * HEAD_WIDTH), MODEL_WIDTH ** -0.5, 0.125, ((0, 8), (1, 4))),
        "gate_weight": normal_values(key_list[5], (MODEL_WIDTH, QUERY_HEADS * HEAD_WIDTH), MODEL_WIDTH ** -0.5, 0.125, ((0, 8), (1, 4))),
        "out_weight": normal_values(key_list[6], (QUERY_HEADS * HEAD_WIDTH, MODEL_WIDTH), (QUERY_HEADS * HEAD_WIDTH // 64) ** -0.5, 1.0, ((0, 4), (1, 8))),
        "ffn_gate_weight": normal_values(key_list[7], (MODEL_WIDTH, FF), MODEL_WIDTH ** -0.5, 0.125, ((0, 8), (1, 4))),
        "ffn_up_weight": normal_values(key_list[8], (MODEL_WIDTH, FF), MODEL_WIDTH ** -0.5, 0.125, ((0, 8), (1, 4))),
        "ffn_down_weight": heavy_noise(key_list[9], (FF, MODEL_WIDTH), FF ** -0.5, 0.109375, ((0, 4), (1, 8)), (0, 1, 8, 2.0)),
        "attn_gain": jnp.clip(1.0 + 0.1 * jax.random.normal(key_list[10], (MODEL_WIDTH,), jnp.float32), 0.5, 1.5),
        "ffn_gain": jnp.clip(1.0 + 0.1 * jax.random.normal(key_list[11], (MODEL_WIDTH,), jnp.float32), 0.5, 1.5),
        "query_gain": jnp.clip(1.0 + 0.18 * jax.random.normal(key_list[12], (HEAD_WIDTH,), jnp.float32), 0.1, 1.9),
        "key_norm_gain": jnp.clip(1.0 + 0.18 * jax.random.normal(key_list[13], (HEAD_WIDTH,), jnp.float32), 0.1, 1.9),
        "cotangent": heavy_noise(key_list[14], (SEQS, SEQ, MODEL_WIDTH), 1.0, 6.0, ((0, 8),), (0, 2, 8, 2.0)),
    }


epsilon = 1e-06
highest_precision = lax.Precision.HIGHEST

@jax.custom_vjp
def reduced_precision(v):
    return lax.optimization_barrier(v.astype(jnp.bfloat16)).astype(jnp.float32)

@jax.custom_vjp
def low_back(v):
    return v

def low_keep(v):
    return (reduced_precision(v), None)

def low_pass(kept, grad):
    return (grad,)

def back_keep(v):
    return (v, None)

def back_low(kept, grad):
    return (reduced_precision(grad),)
reduced_precision.defvjp(low_keep, low_pass)
low_back.defvjp(back_keep, back_low)

def product(left_side, right_side):
    return jnp.dot(left_side, right_side, precision=highest_precision, preferred_element_type=jnp.float32)

def normalized_rows(vector_in):
    return vector_in * lax.rsqrt(lax.optimization_barrier(jnp.mean(vector_in * vector_in, axis=-1, keepdims=True)) + epsilon)

def rotary_apply(vector_in, cosine_table, sine_table):
    halfway = vector_in.shape[-1] // 2
    turned = jnp.concatenate([-vector_in[..., halfway:], vector_in[..., :halfway]], axis=-1)
    return vector_in * cosine_table + turned * sine_table

def tables(segment_row, head_size):
    token_length = segment_row.shape[0]
    places = jnp.arange(token_length, dtype=jnp.int32)
    changed = jnp.concatenate([jnp.ones((1,), dtype=jnp.bool_), segment_row[1:] != segment_row[:-1]])
    starts = lax.cummax(jnp.where(changed, places, jnp.zeros_like(places)), axis=0)
    position = (places - starts).astype(jnp.float32)
    frequency = jnp.exp(jnp.arange(head_size // 2, dtype=jnp.float32) * (-2.0 * math.log(1000000.0) / head_size))
    angles = position[:, None] * frequency[None, :]
    angles = jnp.concatenate([angles, angles], axis=-1)
    allowed = (segment_row[:, None] == segment_row[None, :]) & (places[None, :] <= places[:, None])
    return (jnp.cos(angles)[:, None, :], jnp.sin(angles)[:, None, :], allowed)

def layer_forward(seq_input, weights, cosine_table, sine_table, allowed):
    query_weight, key_matrix, value_matrix, gate_weight, out_weight, ffn_gate_weight, ffn_up_weight, ffn_down_weight, attn_gain, ffn_gain, query_gain, key_norm_gain = weights
    token_length = seq_input.shape[0]
    group_width = QUERY_HEADS // KEY_VALUE_HEADS
    first_normed = reduced_precision(normalized_rows(seq_input) * attn_gain)
    query_proj = low_back(product(first_normed, query_weight))
    key_projected = low_back(product(first_normed, key_matrix))
    value_projected = low_back(product(first_normed, value_matrix))
    gate_proj = low_back(product(first_normed, gate_weight))
    query_rows = reduced_precision(rotary_apply(normalized_rows(query_proj.reshape(token_length, QUERY_HEADS, HEAD_WIDTH)) * query_gain, cosine_table, sine_table))
    key_head_rows = reduced_precision(rotary_apply(normalized_rows(key_projected.reshape(token_length, KEY_VALUE_HEADS, HEAD_WIDTH)) * key_norm_gain, cosine_table, sine_table))
    value_head_rows = reduced_precision(value_projected).reshape(token_length, KEY_VALUE_HEADS, HEAD_WIDTH)
    query_groups = query_rows.reshape(token_length, KEY_VALUE_HEADS, group_width, HEAD_WIDTH)
    raw_scores = low_back(jnp.einsum('skgd,tkd->kgst', query_groups, key_head_rows, precision=highest_precision))
    scores = jnp.where(allowed, raw_scores * HEAD_WIDTH ** (-0.5), -1000000000.0)
    softmaxed = jax.nn.softmax(scores, axis=-1)
    attended = low_back(jnp.einsum('kgst,tkd->skgd', reduced_precision(softmaxed), value_head_rows, precision=highest_precision)).reshape(token_length, QUERY_HEADS * HEAD_WIDTH)
    gated = reduced_precision(low_back(attended * jax.nn.sigmoid(gate_proj)))
    middle = seq_input + low_back(product(gated, out_weight))
    second_normed = reduced_precision(normalized_rows(middle) * ffn_gain)
    ffn_gate = low_back(product(second_normed, ffn_gate_weight))
    ffn_up = low_back(product(second_normed, ffn_up_weight))
    hidden = reduced_precision(jax.nn.silu(ffn_gate) * ffn_up)
    return middle + low_back(product(hidden, ffn_down_weight))

def reference(layer_input, segments, query_weight, key_matrix, value_matrix, gate_weight, out_weight, ffn_gate_weight, ffn_up_weight, ffn_down_weight, attn_gain, ffn_gain, query_gain, key_norm_gain, cotangent):
    weights = tuple((weight.astype(jnp.float32) for weight in (query_weight, key_matrix, value_matrix, gate_weight, out_weight, ffn_gate_weight, ffn_up_weight, ffn_down_weight, attn_gain, ffn_gain, query_gain, key_norm_gain)))
    zero_grads = tuple((jnp.zeros_like(weight) for weight in weights))

    def scan_step(totals, scan_item):
        seq_input, seg_row, seq_cotangent = scan_item
        cosine_table, sine_table, allowed = tables(seg_row, HEAD_WIDTH)
        result, pullback = jax.vjp(lambda input_vals, weight_vals: layer_forward(input_vals, weight_vals, cosine_table, sine_table, allowed), seq_input.astype(jnp.float32), weights)
        grad_input, grad_weights = pullback(seq_cotangent.astype(jnp.float32))
        totals = tuple((running + adding for running, adding in zip(totals, grad_weights)))
        return (totals, (result.astype(jnp.bfloat16), grad_input))
    totals, (results, input_grads) = lax.scan(scan_step, zero_grads, (layer_input, segments, cotangent))
    return (results, input_grads, totals[0], totals[1], totals[2], totals[3], totals[4], totals[5], totals[6], totals[7], totals[8], totals[9], totals[10], totals[11])
```

```python
import math

import jax
import jax.numpy as jnp
from jax import lax
from jax.sharding import PartitionSpec as P

epsilon = 1e-06
low_type = jnp.bfloat16
wide_type = jnp.float32


def norm_fwd(vector_in):
    scale_inv = lax.rsqrt(jnp.mean(vector_in * vector_in, axis=-1, keepdims=True) + epsilon)
    return (vector_in * scale_inv, scale_inv)


def norm_back(normal, scale_inv, gain_vec, grad_in_rows):
    scaled = grad_in_rows * gain_vec
    grad_rows = scale_inv * (scaled - normal * jnp.mean(scaled * normal, axis=-1, keepdims=True))
    return (grad_rows, jnp.sum(grad_in_rows * normal, axis=0))


def rotary_apply(vector_in, cosine_table, sine_table):
    halfway = vector_in.shape[-1] // 2
    turned = jnp.concatenate([-vector_in[..., halfway:], vector_in[..., :halfway]], axis=-1)
    return vector_in * cosine_table + turned * sine_table


def tables(segment_row, head_size):
    token_length = segment_row.shape[0]
    places = jnp.arange(token_length, dtype=jnp.int32)
    changed = jnp.concatenate(
        [jnp.ones((1,), dtype=jnp.bool_), segment_row[1:] != segment_row[:-1]]
    )
    starts = lax.cummax(jnp.where(changed, places, jnp.zeros_like(places)), axis=0)
    position = (places - starts).astype(jnp.float32)
    frequency = jnp.exp(
        jnp.arange(head_size // 2, dtype=jnp.float32) * (-2.0 * math.log(1000000.0) / head_size)
    )
    angles = position[:, None] * frequency[None, :]
    angles = jnp.concatenate([angles, angles], axis=-1)
    allowed = (segment_row[:, None] == segment_row[None, :]) & (places[None, :] <= places[:, None])
    return (jnp.cos(angles)[:, None, :], jnp.sin(angles)[:, None, :], allowed)


def matmul(left, right):
    return jnp.dot(left, right, preferred_element_type=wide_type)


def matmul_nt(left, right):
    return jnp.einsum("tf,df->td", left, right, preferred_element_type=wide_type)


def matmul_tn(left, right):
    return jnp.einsum("td,tf->df", left, right, preferred_element_type=wide_type)


def swap_pairs(size, bit):
    return [(place, place ^ bit) for place in range(size)]


def halves(rows_of, side, extent, axis):
    half = extent // 2
    return (
        lax.dynamic_slice_in_dim(rows_of, (1 - side) * half, half, axis),
        lax.dynamic_slice_in_dim(rows_of, side * half, half, axis),
    )


def tensor_scatter(make, operands, rank, size):
    rows = operands[0].shape[0]
    split = [halves(operand, rank % 2, rows, 0) for operand in operands]
    sent = make(*[pair[0] for pair in split]).astype(low_type)
    received = lax.ppermute(sent, "tensor", swap_pairs(size, 1))
    kept = make(*[pair[1] for pair in split]) + received.astype(wide_type)
    rows, bit = rows // 2, 2
    while bit < size:
        sent, kept = halves(kept, (rank // bit) % 2, rows, 0)
        received = lax.ppermute(sent.astype(low_type), "tensor", swap_pairs(size, bit))
        kept = kept + received.astype(wide_type)
        rows, bit = rows // 2, bit * 2
    return kept


def share_start(rank, size, rows):
    start, bit = 0, 1
    while bit < size:
        rows = rows // 2
        start = start + ((rank // bit) % 2) * rows
        bit = bit * 2
    return start


def tensor_gather(share, rank, size):
    bit = size // 2
    while bit >= 1:
        received = lax.ppermute(share, "tensor", swap_pairs(size, bit))
        low_side = (rank // bit) % 2 == 0
        share = jnp.concatenate(
            [jnp.where(low_side, share, received), jnp.where(low_side, received, share)], axis=0
        )
        bit = bit // 2
    return share


def pair_blocks(activation, rank, inner, outer):
    rows, width = activation.shape
    blocks = activation.reshape(rows, outer, inner, width // (outer * inner))
    side = rank % inner
    return tuple(
        lax.dynamic_index_in_dim(blocks, pick, 2, keepdims=False).reshape(rows, width // inner)
        for pick in (inner - 1 - side, side)
    )


def data_scatter(sent, kept, rank, inner, outer, axis):
    size = inner * outer
    received = lax.ppermute(sent, "dp", swap_pairs(size, 1))
    place = rank // inner
    width = kept.shape[axis] // outer

    def block(which):
        return lax.dynamic_slice_in_dim(kept, which * width, width, axis).astype(
            wide_type
        ) + lax.dynamic_slice_in_dim(received, which * width, width, axis).astype(wide_type)

    arrived = []
    for step in range(1, outer):
        route = [
            (z * inner + x, ((z + step) % outer) * inner + x)
            for z in range(outer)
            for x in range(inner)
        ]
        arrived.append(
            lax.ppermute(block((place + step) % outer).astype(low_type), "dp", route)
        )
    total = block(place)
    for part in arrived:
        total = total + part.astype(wide_type)
    return total


def shards(
    layer_input,
    segments,
    query_weight,
    key_matrix,
    value_matrix,
    gate_weight,
    out_weight,
    ffn_gate_weight,
    ffn_up_weight,
    ffn_down_weight,
    attn_gain,
    ffn_gain,
    query_gain,
    key_norm_gain,
    cotangent,
):
    tensor_rank, tensor_size = lax.axis_index("tensor"), lax.axis_size("tensor")
    data_rank, data_size = lax.axis_index("dp"), lax.axis_size("dp")
    inner = 2
    outer = data_size // inner
    seqs, token_length, width = layer_input.shape
    tokens = seqs * token_length
    head_size = query_gain.shape[0]
    cols_q, cols_k, cols_v = query_weight.shape[1], key_matrix.shape[1], value_matrix.shape[1]
    heads_q, heads_kv = cols_q // head_size, cols_k // head_size
    group_width = heads_q // heads_kv
    scaling = head_size ** (-0.5)

    def gather_rows(shard):
        return lax.all_gather(shard, "dp", axis=0, tiled=True)

    def exchange(sent, kept, axis):
        return data_scatter(sent, kept, data_rank, inner, outer, axis)

    full_in = gather_rows(
        jnp.concatenate([query_weight, key_matrix, value_matrix, gate_weight], axis=1)
    )
    full_o = lax.all_gather(out_weight, "dp", axis=1, tiled=True)
    full_gf = gather_rows(ffn_gate_weight)
    full_up = gather_rows(ffn_up_weight)
    full_dn = lax.all_gather(ffn_down_weight, "dp", axis=1, tiled=True)

    flat_input = layer_input.reshape(tokens, width)
    grad_low = cotangent.reshape(tokens, width)
    first_row = share_start(tensor_rank, tensor_size, tokens)
    share_rows = tokens // tensor_size
    share_input = lax.dynamic_slice_in_dim(flat_input, first_row, share_rows, 0).astype(wide_type)
    share_cotangent = lax.dynamic_slice_in_dim(grad_low, first_row, share_rows, 0).astype(
        wide_type
    )

    cosine_table, sine_table, allowed = jax.vmap(lambda row: tables(row, head_size))(segments)
    allowed = allowed[:, None, None]
    first_normed = (norm_fwd(flat_input.astype(wide_type))[0] * attn_gain).astype(low_type)
    projected = matmul(first_normed, full_in)
    query_proj = projected[:, :cols_q]
    key_proj = projected[:, cols_q : cols_q + cols_k]
    value_proj = projected[:, cols_q + cols_k : cols_q + cols_k + cols_v]
    gate_proj = projected[:, cols_q + cols_k + cols_v :]

    def prepare(query_in, key_in, gain_q, gain_k):
        query_n = norm_fwd(query_in.reshape(seqs, token_length, heads_q, head_size))[0] * gain_q
        key_n = norm_fwd(key_in.reshape(seqs, token_length, heads_kv, head_size))[0] * gain_k
        return (
            rotary_apply(query_n, cosine_table, sine_table),
            rotary_apply(key_n, cosine_table, sine_table),
        )

    (query_full, key_full), prepare_back = jax.vjp(
        prepare, query_proj, key_proj, query_gain, key_norm_gain
    )
    query_low = query_full.astype(low_type).reshape(
        seqs, token_length, heads_kv, group_width, head_size
    )
    key_low = key_full.astype(low_type)
    value_low = value_proj.astype(low_type).reshape(seqs, token_length, heads_kv, head_size)
    raw_scores = jnp.einsum(
        "bskgd,btkd->bkgst", query_low, key_low, preferred_element_type=wide_type
    )
    scores = jnp.where(allowed, raw_scores * scaling, -1000000000.0)
    highest = jnp.max(scores, axis=-1, keepdims=True)
    exponent = jnp.exp(scores - highest)
    softmaxed = exponent / jnp.sum(exponent, axis=-1, keepdims=True)
    probs_low = softmaxed.astype(low_type)
    attended = jnp.einsum(
        "bkgst,btkd->bskgd", probs_low, value_low, preferred_element_type=wide_type
    ).reshape(tokens, cols_q)
    gate_sig = jax.nn.sigmoid(gate_proj)
    gated = (attended * gate_sig).astype(low_type)

    branch_one = tensor_scatter(
        lambda rows: matmul(rows, full_o), (gated,), tensor_rank, tensor_size
    )
    middle = share_input + branch_one
    normal_two, inv_two = norm_fwd(middle)
    second_normed = tensor_gather(
        (normal_two * ffn_gain).astype(low_type), tensor_rank, tensor_size
    )
    ffn_gate = matmul(second_normed, full_gf)
    ffn_up = matmul(second_normed, full_up)
    sig_gate = jax.nn.sigmoid(ffn_gate)
    active = ffn_gate * sig_gate
    hidden = (active * ffn_up).astype(low_type)
    branch_two = tensor_scatter(
        lambda rows: matmul(rows, full_dn), (hidden,), tensor_rank, tensor_size
    )
    result = tensor_gather((middle + branch_two).astype(low_type), tensor_rank, tensor_size)

    low_sent, low_kept = pair_blocks(grad_low, data_rank, inner, outer)
    grad_dn = exchange(
        matmul_tn(hidden, low_sent).astype(low_type),
        matmul_tn(hidden, low_kept).astype(low_type),
        1,
    )
    grad_hidden = matmul_nt(grad_low, full_dn)
    grad_ffn_gate = (grad_hidden * ffn_up * sig_gate * (1.0 + ffn_gate * (1.0 - sig_gate))).astype(
        low_type
    )
    grad_ffn_up = (grad_hidden * active).astype(low_type)
    grad_second = tensor_scatter(
        lambda gate_rows, up_rows: matmul_nt(gate_rows, full_gf) + matmul_nt(up_rows, full_up),
        (grad_ffn_gate, grad_ffn_up),
        tensor_rank,
        tensor_size,
    )
    second_sent, second_kept = pair_blocks(second_normed, data_rank, inner, outer)
    grad_gf = exchange(
        matmul_tn(second_sent, grad_ffn_gate).astype(low_type),
        matmul_tn(second_kept, grad_ffn_gate).astype(low_type),
        0,
    )
    grad_up = exchange(
        matmul_tn(second_sent, grad_ffn_up).astype(low_type),
        matmul_tn(second_kept, grad_ffn_up).astype(low_type),
        0,
    )
    back_two, grad_ffn_gain = norm_back(normal_two, inv_two, ffn_gain, grad_second)
    grad_middle = share_cotangent + back_two
    middle_low = tensor_gather(grad_middle.astype(low_type), tensor_rank, tensor_size)

    grad_gated = matmul_nt(middle_low, full_o).astype(low_type).astype(wide_type)
    grad_attended = (
        (grad_gated * gate_sig)
        .astype(low_type)
        .reshape(seqs, token_length, heads_kv, group_width, head_size)
    )
    grad_gate_proj = (grad_gated * attended * gate_sig * (1.0 - gate_sig)).astype(low_type)
    middle_sent, middle_kept = pair_blocks(middle_low, data_rank, inner, outer)
    grad_o = exchange(
        matmul_tn(gated, middle_sent).astype(low_type),
        matmul_tn(gated, middle_kept).astype(low_type),
        1,
    )
    first_sent, first_kept = pair_blocks(first_normed, data_rank, inner, outer)
    grad_g = exchange(
        matmul_tn(first_sent, grad_gate_proj).astype(low_type),
        matmul_tn(first_kept, grad_gate_proj).astype(low_type),
        0,
    )
    grad_value = (
        jnp.einsum(
            "bkgst,bskgd->btkd", probs_low, grad_attended, preferred_element_type=wide_type
        )
        .astype(low_type)
        .reshape(tokens, cols_v)
    )
    grad_probs = jnp.einsum(
        "bskgd,btkd->bkgst", grad_attended, value_low, preferred_element_type=wide_type
    )
    grad_scores = (
        softmaxed * (grad_probs - jnp.sum(softmaxed * grad_probs, axis=-1, keepdims=True)) * scaling
    ).astype(low_type)
    grad_queries = jnp.einsum(
        "bkgst,btkd->bskgd", grad_scores, key_low, preferred_element_type=wide_type
    ).reshape(seqs, token_length, heads_q, head_size)
    grad_keys = jnp.einsum(
        "bkgst,bskgd->btkd", grad_scores, query_low, preferred_element_type=wide_type
    )
    grad_query_proj, grad_key_proj, grad_query_gain, grad_key_gain = prepare_back(
        (grad_queries, grad_keys)
    )
    grad_qkv = jnp.concatenate(
        [grad_query_proj.astype(low_type), grad_key_proj.astype(low_type), grad_value], axis=1
    )
    grads_qkv = exchange(
        matmul_tn(first_sent, grad_qkv).astype(low_type),
        matmul_tn(first_kept, grad_qkv).astype(low_type),
        0,
    )
    cols_qkv = cols_q + cols_k + cols_v
    grad_first = tensor_scatter(
        lambda qkv_rows, gate_rows: matmul_nt(qkv_rows, full_in[:, :cols_qkv])
        + matmul_nt(gate_rows, full_in[:, cols_qkv:]),
        (grad_qkv, grad_gate_proj),
        tensor_rank,
        tensor_size,
    )
    normal_one, inv_one = norm_fwd(share_input)
    back_one, grad_attn_gain = norm_back(normal_one, inv_one, attn_gain, grad_first)
    grad_input = tensor_gather(
        (grad_middle + back_one).astype(low_type), tensor_rank, tensor_size
    ).astype(wide_type)

    gains = jnp.concatenate([grad_attn_gain, grad_ffn_gain, grad_query_gain, grad_key_gain])
    for axis_name, size in (("tensor", tensor_size), ("dp", data_size)):
        bit = 1
        while bit < size:
            gains = gains + lax.ppermute(gains, axis_name, swap_pairs(size, bit))
            bit = bit * 2
    return (
        result.reshape(seqs, token_length, width),
        grad_input.reshape(seqs, token_length, width),
        grads_qkv[:, :cols_q],
        grads_qkv[:, cols_q : cols_q + cols_k],
        grads_qkv[:, cols_q + cols_k :],
        grad_g,
        grad_o,
        grad_gf,
        grad_up,
        grad_dn,
        gains[:width],
        gains[width : 2 * width],
        gains[2 * width : 2 * width + head_size],
        gains[2 * width + head_size :],
    )


def solution(mesh):
    return jax.shard_map(
        shards,
        mesh=mesh,
        in_specs=(
            P("dp", None, None),
            P("dp", None),
            P("dp", "tensor"),
            P("dp", "tensor"),
            P("dp", "tensor"),
            P("dp", "tensor"),
            P("tensor", "dp"),
            P("dp", "tensor"),
            P("dp", "tensor"),
            P("tensor", "dp"),
            P(),
            P(),
            P(),
            P(),
            P("dp", None, None),
        ),
        out_specs=(
            P("dp", None, None),
            P("dp", None, None),
            P("dp", "tensor"),
            P("dp", "tensor"),
            P("dp", "tensor"),
            P("dp", "tensor"),
            P("tensor", "dp"),
            P("dp", "tensor"),
            P("dp", "tensor"),
            P("tensor", "dp"),
            P(),
            P(),
            P(),
            P(),
        ),
        check_vma=False,
    )
```

```python
import math

import jax
import jax.numpy as jnp
from jax import lax
from jax.experimental import pallas as pl
from jax.experimental.pallas import tpu as pltpu
from jax.sharding import PartitionSpec as P

epsilon = 1e-06
low_type = jnp.bfloat16
wide_type = jnp.float32


def norm_fwd(vector_in):
    scale_inv = lax.rsqrt(jnp.mean(vector_in * vector_in, axis=-1, keepdims=True) + epsilon)
    return (vector_in * scale_inv, scale_inv)


def norm_back(normal, scale_inv, gain_vec, grad_in_rows):
    scaled = grad_in_rows * gain_vec
    grad_rows = scale_inv * (scaled - normal * jnp.mean(scaled * normal, axis=-1, keepdims=True))
    return (grad_rows, jnp.sum(grad_in_rows * normal, axis=0))


def tables(segment_row, head_size):
    token_length = segment_row.shape[0]
    places = jnp.arange(token_length, dtype=jnp.int32)
    changed = jnp.concatenate(
        [jnp.ones((1,), dtype=jnp.bool_), segment_row[1:] != segment_row[:-1]]
    )
    starts = lax.cummax(jnp.where(changed, places, jnp.zeros_like(places)), axis=0)
    position = (places - starts).astype(jnp.float32)
    frequency = jnp.exp(
        jnp.arange(head_size // 2, dtype=jnp.float32) * (-2.0 * math.log(1000000.0) / head_size)
    )
    angles = position[:, None] * frequency[None, :]
    sine = jnp.sin(angles)
    return (
        jnp.concatenate([jnp.cos(angles), jnp.cos(angles)], axis=-1),
        jnp.concatenate([-sine, sine], axis=-1),
    )


def head_norm(projected):
    inverse = lax.rsqrt(jnp.mean(projected * projected, axis=-1, keepdims=True) + epsilon)
    return projected * inverse, inverse


def rotate(rows, cosine, signed_sine):
    return rows * cosine + pltpu.roll(rows, rows.shape[-1] // 2, 1) * signed_sine


def rotate_back(grad, cosine, signed_sine):
    return grad * cosine + pltpu.roll(grad * signed_sine, grad.shape[-1] // 2, 1)


def norm_rows_back(normal, inverse, gain, grad):
    scaled = grad * gain
    return inverse * (scaled - normal * jnp.mean(scaled * normal, axis=-1, keepdims=True))


def dot_nt(left, right):
    return lax.dot_general(left, right, (((1,), (1,)), ((), ())), preferred_element_type=wide_type)


def dot_tn(left, right):
    return lax.dot_general(left, right, (((0,), (0,)), ((), ())), preferred_element_type=wide_type)


def allowed_pairs(seg_col, seg_row):
    shape = (seg_col.shape[0], seg_row.shape[1])
    later = lax.broadcasted_iota(jnp.int32, shape, 0) >= lax.broadcasted_iota(jnp.int32, shape, 1)
    return (seg_col == seg_row) & later


def softmax_rows(query, key, allowed, scaling):
    scores = jnp.where(allowed, dot_nt(query, key) * scaling, -1000000000.0)
    exponent = jnp.exp(scores - jnp.max(scores, axis=-1, keepdims=True))
    return exponent / jnp.sum(exponent, axis=-1, keepdims=True)


def attention_forward(
    q_ref, k_ref, v_ref, g_ref, cos_ref, sin_ref, col_ref, row_ref, gq_ref, gk_ref, out_ref
):
    head = k_ref.shape[1]
    scaling = head ** (-0.5)
    cosine, sine = cos_ref[...], sin_ref[...]
    allowed = allowed_pairs(col_ref[0], row_ref[0])
    key = rotate(head_norm(k_ref[...])[0] * gk_ref[...], cosine, sine).astype(low_type)
    value = v_ref[...].astype(low_type)
    for member in range(q_ref.shape[1] // head):
        cols = pl.ds(member * head, head)
        query = rotate(head_norm(q_ref[:, cols])[0] * gq_ref[...], cosine, sine).astype(low_type)
        probs = softmax_rows(query, key, allowed, scaling).astype(low_type)
        attended = jnp.dot(probs, value, preferred_element_type=wide_type)
        out_ref[:, cols] = (attended * jax.nn.sigmoid(g_ref[:, cols])).astype(low_type)


def attention_backward(
    q_ref,
    k_ref,
    v_ref,
    g_ref,
    cos_ref,
    sin_ref,
    col_ref,
    row_ref,
    gq_ref,
    gk_ref,
    grad_ref,
    dq_ref,
    dk_ref,
    dv_ref,
    dg_ref,
    gain_ref,
):
    head = k_ref.shape[1]
    scaling = head ** (-0.5)
    cosine, sine = cos_ref[...], sin_ref[...]
    allowed = allowed_pairs(col_ref[0], row_ref[0])
    key_normal, key_inverse = head_norm(k_ref[...])
    key = rotate(key_normal * gk_ref[...], cosine, sine).astype(low_type)
    value = v_ref[...].astype(low_type)
    grad_value = jnp.zeros(value.shape, wide_type)
    grad_key = jnp.zeros(value.shape, wide_type)
    query_gain = jnp.zeros((1, head), wide_type)
    for member in range(q_ref.shape[1] // head):
        cols = pl.ds(member * head, head)
        query_normal, query_inverse = head_norm(q_ref[:, cols])
        query = rotate(query_normal * gq_ref[...], cosine, sine).astype(low_type)
        probs = softmax_rows(query, key, allowed, scaling)
        probs_low = probs.astype(low_type)
        attended = jnp.dot(probs_low, value, preferred_element_type=wide_type)
        gate = jax.nn.sigmoid(g_ref[:, cols])
        grad_gated = grad_ref[:, cols].astype(wide_type)
        grad_attended = (grad_gated * gate).astype(low_type)
        dg_ref[:, cols] = (grad_gated * attended * gate * (1.0 - gate)).astype(low_type)
        grad_value = grad_value + dot_tn(probs_low, grad_attended)
        grad_probs = dot_nt(grad_attended, value)
        mixed = jnp.sum(probs * grad_probs, axis=-1, keepdims=True)
        grad_scores = (probs * (grad_probs - mixed) * scaling).astype(low_type)
        grad_query = rotate_back(
            jnp.dot(grad_scores, key, preferred_element_type=wide_type), cosine, sine
        )
        grad_key = grad_key + dot_tn(grad_scores, query)
        query_gain = query_gain + jnp.sum(grad_query * query_normal, axis=0, keepdims=True)
        dq_ref[:, cols] = norm_rows_back(
            query_normal, query_inverse, gq_ref[...], grad_query
        ).astype(low_type)
    grad_key = rotate_back(grad_key, cosine, sine)
    dk_ref[...] = norm_rows_back(key_normal, key_inverse, gk_ref[...], grad_key).astype(low_type)
    dv_ref[...] = grad_value.astype(low_type)
    gain_ref[0, 0, 0:1] = query_gain
    gain_ref[0, 0, 1:2] = jnp.sum(grad_key * key_normal, axis=0, keepdims=True)


def attention_specs(length, head, group, kv_heads):
    wide = group * head
    specs = [
        pl.BlockSpec((length, wide), lambda s, k: (s, k)),
        pl.BlockSpec((length, head), lambda s, k: (s, kv_heads * group + k)),
        pl.BlockSpec((length, head), lambda s, k: (s, kv_heads * (group + 1) + k)),
        pl.BlockSpec((length, wide), lambda s, k: (s, kv_heads * (group + 2) // group + k)),
        pl.BlockSpec((length, head), lambda s, k: (s, 0)),
        pl.BlockSpec((length, head), lambda s, k: (s, 0)),
        pl.BlockSpec((1, length, 1), lambda s, k: (s, 0, 0)),
        pl.BlockSpec((1, 1, length), lambda s, k: (s, 0, 0)),
        pl.BlockSpec((1, head), lambda s, k: (0, 0)),
        pl.BlockSpec((1, head), lambda s, k: (0, 0)),
    ]
    return specs, specs[0], pl.BlockSpec((length, head), lambda s, k: (s, k))


def attention_calls(seqs, length, head, group, kv_heads, interpret=False):
    specs, wide_spec, head_spec = attention_specs(length, head, group, kv_heads)
    tokens = seqs * length
    wide = jax.ShapeDtypeStruct((tokens, kv_heads * group * head), low_type)
    narrow = jax.ShapeDtypeStruct((tokens, kv_heads * head), low_type)
    gains = jax.ShapeDtypeStruct((seqs, kv_heads, 2, head), wide_type)
    forward = pl.pallas_call(
        attention_forward,
        grid=(seqs, kv_heads),
        in_specs=specs,
        out_specs=wide_spec,
        out_shape=wide,
        interpret=interpret,
    )
    backward = pl.pallas_call(
        attention_backward,
        grid=(seqs, kv_heads),
        in_specs=specs + [wide_spec],
        out_specs=[
            wide_spec,
            head_spec,
            head_spec,
            wide_spec,
            pl.BlockSpec((1, 1, 2, head), lambda s, k: (s, k, 0, 0)),
        ],
        out_shape=[wide, narrow, narrow, wide, gains],
        interpret=interpret,
    )
    return forward, backward


def transpose_block(in_ref, out_ref):
    out_ref[...] = in_ref[...].T


def turned(grad):
    rows, cols = grad.shape
    step = min(cols, 256)
    return pl.pallas_call(
        transpose_block,
        grid=(cols // step,),
        in_specs=[pl.BlockSpec((rows, step), lambda i: (0, i))],
        out_specs=pl.BlockSpec((step, rows), lambda i: (i, 0)),
        out_shape=jax.ShapeDtypeStruct((cols, rows), grad.dtype),
    )(grad)


def matmul(left, right):
    return jnp.dot(left, right, preferred_element_type=wide_type)


def matmul_nt(left, right):
    return jnp.einsum("tf,df->td", left, right, preferred_element_type=wide_type)


def matmul_tn(left, right):
    return jnp.einsum("td,tf->df", left, right, preferred_element_type=wide_type)


def swap_pairs(size, bit):
    return [(place, place ^ bit) for place in range(size)]


def after(value, *earlier):
    return lax.optimization_barrier((value,) + earlier)[0] if earlier else value


def halves(rows_of, side, extent, axis):
    half = extent // 2
    return (
        lax.dynamic_slice_in_dim(rows_of, (1 - side) * half, half, axis),
        lax.dynamic_slice_in_dim(rows_of, side * half, half, axis),
    )


def tensor_scatter(make, operands, rank, size, fill=()):
    rows = operands[0].shape[0]
    split = [halves(operand, rank % 2, rows, 0) for operand in operands]
    sent = make(*[pair[0] for pair in split]).astype(low_type)
    received = lax.ppermute(sent, "tensor", swap_pairs(size, 1))
    kept = make(*[pair[1] for pair in split])
    kept = kept + after(received, kept).astype(wide_type)
    rows, bit = rows // 2, 2
    while bit < size:
        sent, kept = halves(kept, (rank // bit) % 2, rows, 0)
        received = lax.ppermute(sent.astype(low_type), "tensor", swap_pairs(size, bit))
        kept = kept + after(received, *fill).astype(wide_type)
        rows, bit = rows // 2, bit * 2
    return kept


def share_start(rank, size, rows):
    start, bit = 0, 1
    while bit < size:
        rows = rows // 2
        start = start + ((rank // bit) % 2) * rows
        bit = bit * 2
    return start


def tensor_gather(share, rank, size, fill=()):
    bit = size // 2
    while bit >= 1:
        received = lax.ppermute(share, "tensor", swap_pairs(size, bit))
        received = after(received, *fill) if bit > 1 else received
        low_side = (rank // bit) % 2 == 0
        share = jnp.concatenate(
            [jnp.where(low_side, share, received), jnp.where(low_side, received, share)], axis=0
        )
        bit = bit // 2
    return share


def outer_route(step, inner, outer):
    return [
        (z * inner + x, ((z + step) % outer) * inner + x)
        for z in range(outer)
        for x in range(inner)
    ]


def line_send(shard, inner, outer):
    return [
        lax.ppermute(shard, "dp", outer_route(step, inner, outer)) for step in range(1, outer)
    ]


def line_join(shard, arrived, rank, inner, outer):
    place = rank // inner
    line = lax.dynamic_update_slice_in_dim(
        jnp.zeros((outer,) + shard.shape, shard.dtype), shard[None], place, 0
    )
    for step in range(1, outer):
        line = lax.dynamic_update_slice_in_dim(
            line, arrived[step - 1][None], (place - step) % outer, 0
        )
    return line


def pair_send(line, inner, outer):
    return lax.ppermute(line, "dp", swap_pairs(inner * outer, 1))


def in_order(line, other, rank, inner):
    side = rank % inner
    return jnp.where(side == 0, line, other), jnp.where(side == 0, other, line)


def join_rows(pair):
    outer, rows, cols = pair[0].shape
    return jnp.stack(pair, axis=1).reshape(outer * len(pair) * rows, cols)


def join_columns(pair):
    return jnp.concatenate([part[z] for z in range(pair[0].shape[0]) for part in pair], axis=1)


def scatter_send(grad, rank, inner, outer):
    rows = grad.shape[0] // (inner * outer)
    blocks = grad.reshape(outer, inner, rows, grad.shape[1])
    sent = lax.dynamic_index_in_dim(blocks, 1 - rank % inner, 1, keepdims=False)
    return blocks, lax.ppermute(sent, "dp", swap_pairs(inner * outer, 1))


def scatter_line(blocks, received, rank, inner, outer):
    place, side = rank // inner, rank % inner
    rows, cols = blocks.shape[2:]

    def block(which):
        mine = lax.dynamic_slice(blocks, (which, side, 0, 0), (1, 1, rows, cols))
        theirs = lax.dynamic_index_in_dim(received, which, 0, keepdims=False)
        return mine.reshape(rows, cols).astype(wide_type) + theirs.astype(wide_type)

    arrived = tuple(
        lax.ppermute(
            block((place + step) % outer).astype(low_type), "dp", outer_route(step, inner, outer)
        )
        for step in range(1, outer)
    )
    return block(place), arrived


def scatter_sum(total, arrived, *earlier):
    if earlier:
        arrived = lax.optimization_barrier(tuple(arrived) + earlier)[: len(arrived)]
    for part in arrived:
        total = total + part.astype(wide_type)
    return total


def shards(
    layer_input,
    segments,
    query_weight,
    key_matrix,
    value_matrix,
    gate_weight,
    out_weight,
    ffn_gate_weight,
    ffn_up_weight,
    ffn_down_weight,
    attn_gain,
    ffn_gain,
    query_gain,
    key_norm_gain,
    cotangent,
):
    tensor_rank, tensor_size = lax.axis_index("tensor"), lax.axis_size("tensor")
    data_rank, data_size = lax.axis_index("dp"), lax.axis_size("dp")
    inner = 2
    outer = data_size // inner
    seqs, token_length, width = layer_input.shape
    tokens = seqs * token_length
    head_size = query_gain.shape[0]
    cols_q, cols_k, cols_v = query_weight.shape[1], key_matrix.shape[1], value_matrix.shape[1]
    heads_q, heads_kv = cols_q // head_size, cols_k // head_size
    group_width = heads_q // heads_kv

    ring = (data_rank, inner, outer)
    sizes = (inner, outer)
    shard_in = jnp.concatenate([query_weight, key_matrix, value_matrix, gate_weight], axis=1)
    sent_in = line_send(shard_in, *sizes)
    sent_o = line_send(out_weight, *sizes)
    sent_gf = line_send(ffn_gate_weight, *sizes)
    sent_up = line_send(ffn_up_weight, *sizes)
    sent_dn = line_send(ffn_down_weight, *sizes)

    flat_input = layer_input.reshape(tokens, width)
    grad_low = cotangent.reshape(tokens, width)
    first_row = share_start(tensor_rank, tensor_size, tokens)
    share_rows = tokens // tensor_size
    share_input = lax.dynamic_slice_in_dim(flat_input, first_row, share_rows, 0).astype(wide_type)
    share_cotangent = lax.dynamic_slice_in_dim(grad_low, first_row, share_rows, 0).astype(
        wide_type
    )

    cosine_table, sine_table = jax.vmap(lambda row: tables(row, head_size))(segments)
    first_normed = (norm_fwd(flat_input.astype(wide_type))[0] * attn_gain).astype(low_type)
    line_in = line_join(shard_in, sent_in, *ring)
    other_in = pair_send(line_in, *sizes)
    line_o = line_join(out_weight, after(tuple(sent_o), line_in), *ring)
    other_o = pair_send(line_o, *sizes)
    full_in = join_rows(in_order(line_in, after(other_in, line_o, first_normed), data_rank, inner))
    projected = matmul(first_normed, full_in)
    line_gf = line_join(ffn_gate_weight, after(tuple(sent_gf), projected), *ring)
    other_gf = pair_send(line_gf, *sizes)
    attend, attend_back = attention_calls(seqs, token_length, head_size, group_width, heads_kv)
    attend_args = (
        projected,
        projected,
        projected,
        projected,
        cosine_table.reshape(tokens, head_size),
        sine_table.reshape(tokens, head_size),
        segments[:, :, None],
        segments[:, None, :],
        query_gain[None],
        key_norm_gain[None],
    )
    gated = attend(*attend_args)
    full_o = join_columns(in_order(line_o, other_o, data_rank, inner))
    line_up = line_join(ffn_up_weight, after(tuple(sent_up), gated), *ring)
    other_up = pair_send(line_up, *sizes)
    branch_one = tensor_scatter(
        lambda rows: matmul(rows, full_o), (gated,), tensor_rank, tensor_size
    )
    middle = share_input + branch_one
    normal_two, inv_two = norm_fwd(middle)
    second_normed = tensor_gather(
        (normal_two * ffn_gain).astype(low_type), tensor_rank, tensor_size
    )
    line_dn = line_join(ffn_down_weight, after(tuple(sent_dn), second_normed), *ring)
    other_dn = pair_send(line_dn, *sizes)
    full_gf = join_rows(
        in_order(line_gf, after(other_gf, second_normed), data_rank, inner)
    )
    ffn_gate = matmul(second_normed, full_gf)
    full_up = join_rows(in_order(line_up, after(other_up, ffn_gate, line_dn), data_rank, inner))
    ffn_up = matmul(second_normed, full_up)
    sig_gate = jax.nn.sigmoid(ffn_gate)
    active = ffn_gate * sig_gate
    hidden = (active * ffn_up).astype(low_type)
    blocks_dn, pair_dn = scatter_send(matmul_tn(grad_low, hidden).astype(low_type), *ring)
    full_dn = join_columns(in_order(line_dn, after(other_dn, blocks_dn), data_rank, inner))
    grad_hidden = matmul_nt(grad_low, full_dn)
    grad_ffn_gate = (grad_hidden * ffn_up * sig_gate * (1.0 + ffn_gate * (1.0 - sig_gate))).astype(
        low_type
    )
    grad_ffn_up = (grad_hidden * active).astype(low_type)
    weight_gf = matmul_tn(second_normed, grad_ffn_gate).astype(low_type)
    weight_up = matmul_tn(second_normed, grad_ffn_up).astype(low_type)
    blocks_gf, pair_gf = scatter_send(weight_gf, *ring)
    blocks_up, pair_up = scatter_send(weight_up, *ring)
    grad_second = tensor_scatter(
        lambda gate_rows, up_rows: matmul_nt(gate_rows, full_gf) + matmul_nt(up_rows, full_up),
        (grad_ffn_gate, grad_ffn_up),
        tensor_rank,
        tensor_size,
        (weight_gf,),
    )
    back_two, grad_ffn_gain = norm_back(normal_two, inv_two, ffn_gain, grad_second)
    grad_middle = share_cotangent + back_two
    share_low = grad_middle.astype(low_type)
    mine_dn, line_sum_dn = scatter_line(blocks_dn, after(pair_dn, share_low), *ring)
    middle_low = tensor_gather(share_low, tensor_rank, tensor_size, (weight_up, mine_dn))

    grad_gated = matmul_nt(middle_low, full_o).astype(low_type)
    blocks_o, pair_o = scatter_send(matmul_tn(middle_low, gated).astype(low_type), *ring)
    grad_query, grad_key, grad_value, grad_gate_proj, head_gains = attend_back(
        *attend_args, grad_gated
    )
    head_gains = jnp.sum(head_gains, axis=(0, 1))
    grad_qk = jnp.concatenate([grad_query, grad_key], axis=1)
    grad_vg = jnp.concatenate([grad_value, grad_gate_proj], axis=1)
    mine_gf, line_sum_gf = scatter_line(blocks_gf, after(pair_gf, grad_query), *ring)
    weight_vg = matmul_tn(first_normed, grad_vg).astype(low_type)
    weight_qk = matmul_tn(first_normed, grad_qk).astype(low_type)
    blocks_vg, pair_vg = scatter_send(weight_vg, *ring)
    blocks_qk, pair_qk = scatter_send(weight_qk, *ring)
    grad_first = tensor_scatter(
        lambda qk_rows, vg_rows: matmul_nt(qk_rows, full_in[:, : cols_q + cols_k])
        + matmul_nt(vg_rows, full_in[:, cols_q + cols_k :]),
        (grad_qk, grad_vg),
        tensor_rank,
        tensor_size,
        (weight_vg, weight_qk),
    )
    branch_two = tensor_scatter(
        lambda rows: matmul(rows, full_dn),
        (after(hidden, weight_vg, weight_qk),),
        tensor_rank,
        tensor_size,
    )
    result = tensor_gather((middle + branch_two).astype(low_type), tensor_rank, tensor_size)
    mine_up, line_sum_up = scatter_line(blocks_up, after(pair_up, grad_first), *ring)
    mine_o, line_sum_o = scatter_line(blocks_o, after(pair_o, mine_up), *ring)
    mine_vg, line_sum_vg = scatter_line(blocks_vg, after(pair_vg, mine_o), *ring)
    mine_qk, line_sum_qk = scatter_line(blocks_qk, after(pair_qk, mine_vg), *ring)
    grad_dn = turned(scatter_sum(mine_dn, line_sum_dn, mine_up))
    grad_gf = scatter_sum(mine_gf, line_sum_gf, mine_up)
    grad_up = scatter_sum(mine_up, line_sum_up, mine_vg)
    grad_o = turned(scatter_sum(mine_o, line_sum_o, mine_qk))
    grads_vg = scatter_sum(mine_vg, line_sum_vg, mine_qk)
    grads_qk = scatter_sum(mine_qk, line_sum_qk)
    normal_one, inv_one = norm_fwd(share_input)
    back_one, grad_attn_gain = norm_back(normal_one, inv_one, attn_gain, grad_first)
    grad_input = tensor_gather(
        (grad_middle + back_one).astype(low_type), tensor_rank, tensor_size
    ).astype(wide_type)

    gains = jnp.concatenate([grad_attn_gain, grad_ffn_gain, head_gains[0], head_gains[1]])
    for axis_name, size in (("tensor", tensor_size), ("dp", data_size)):
        bit = 1
        while bit < size:
            gains = gains + lax.ppermute(gains, axis_name, swap_pairs(size, bit))
            bit = bit * 2
    return (
        result.reshape(seqs, token_length, width),
        grad_input.reshape(seqs, token_length, width),
        grads_qk[:, :cols_q],
        grads_qk[:, cols_q:],
        grads_vg[:, :cols_v],
        grads_vg[:, cols_v:],
        grad_o,
        grad_gf,
        grad_up,
        grad_dn,
        gains[:width],
        gains[width : 2 * width],
        gains[2 * width : 2 * width + head_size],
        gains[2 * width + head_size :],
    )


def solution(mesh):
    return jax.shard_map(
        shards,
        mesh=mesh,
        in_specs=(
            P("dp", None, None),
            P("dp", None),
            P("dp", "tensor"),
            P("dp", "tensor"),
            P("dp", "tensor"),
            P("dp", "tensor"),
            P("tensor", "dp"),
            P("dp", "tensor"),
            P("dp", "tensor"),
            P("tensor", "dp"),
            P(),
            P(),
            P(),
            P(),
            P("dp", None, None),
        ),
        out_specs=(
            P("dp", None, None),
            P("dp", None, None),
            P("dp", "tensor"),
            P("dp", "tensor"),
            P("dp", "tensor"),
            P("dp", "tensor"),
            P("tensor", "dp"),
            P("dp", "tensor"),
            P("dp", "tensor"),
            P("tensor", "dp"),
            P(),
            P(),
            P(),
            P(),
        ),
        check_vma=False,
    )
```

```python
import math

import jax
import jax.numpy as jnp
from jax import lax
from jax.experimental import pallas as pl
from jax.experimental.pallas import tpu as pltpu
from jax.sharding import PartitionSpec as P


epsilon = 1e-06
low_type = jnp.bfloat16
wide_type = jnp.float32


def norm_fwd(vector_in):
    scale_inv = lax.rsqrt(jnp.mean(vector_in * vector_in, axis=-1, keepdims=True) + epsilon)
    return (vector_in * scale_inv, scale_inv)


def norm_back(normal, scale_inv, gain_vec, grad_in_rows):
    scaled = grad_in_rows * gain_vec
    grad_rows = scale_inv * (scaled - normal * jnp.mean(scaled * normal, axis=-1, keepdims=True))
    return (grad_rows, jnp.sum(grad_in_rows * normal, axis=0))


def tables(segment_row, head_size):
    token_length = segment_row.shape[0]
    places = jnp.arange(token_length, dtype=jnp.int32)
    changed = jnp.concatenate(
        [jnp.ones((1,), dtype=jnp.bool_), segment_row[1:] != segment_row[:-1]]
    )
    starts = lax.cummax(jnp.where(changed, places, jnp.zeros_like(places)), axis=0)
    position = (places - starts).astype(jnp.float32)
    frequency = jnp.exp(
        jnp.arange(head_size // 2, dtype=jnp.float32) * (-2.0 * math.log(1000000.0) / head_size)
    )
    angles = position[:, None] * frequency[None, :]
    sine = jnp.sin(angles)
    return (
        jnp.concatenate([jnp.cos(angles), jnp.cos(angles)], axis=-1),
        jnp.concatenate([-sine, sine], axis=-1),
    )


def head_norm(projected):
    inverse = lax.rsqrt(jnp.mean(projected * projected, axis=-1, keepdims=True) + epsilon)
    return projected * inverse, inverse


def rotate(rows, cosine, signed_sine):
    return rows * cosine + pltpu.roll(rows, rows.shape[-1] // 2, 1) * signed_sine


def rotate_back(grad, cosine, signed_sine):
    return grad * cosine + pltpu.roll(grad * signed_sine, grad.shape[-1] // 2, 1)


def norm_rows_back(normal, inverse, gain, grad):
    scaled = grad * gain
    return inverse * (scaled - normal * jnp.mean(scaled * normal, axis=-1, keepdims=True))


def dot_nt(left, right):
    return lax.dot_general(left, right, (((1,), (1,)), ((), ())), preferred_element_type=wide_type)


def dot_tn(left, right):
    return lax.dot_general(left, right, (((0,), (0,)), ((), ())), preferred_element_type=wide_type)


def allowed_pairs(seg_col, seg_row):
    shape = (seg_col.shape[0], seg_row.shape[1])
    later = lax.broadcasted_iota(jnp.int32, shape, 0) >= lax.broadcasted_iota(jnp.int32, shape, 1)
    return (seg_col == seg_row) & later


def softmax_rows(query, key, allowed, scaling):
    scores = jnp.where(allowed, dot_nt(query, key) * scaling, -1000000000.0)
    exponent = jnp.exp(scores - jnp.max(scores, axis=-1, keepdims=True))
    return exponent / jnp.sum(exponent, axis=-1, keepdims=True)


def attention_forward(
    q_ref, k_ref, v_ref, g_ref, cos_ref, sin_ref, col_ref, row_ref, gq_ref, gk_ref, out_ref
):
    head = k_ref.shape[1]
    scaling = head ** (-0.5)
    cosine, sine = cos_ref[...], sin_ref[...]
    allowed = allowed_pairs(col_ref[0], row_ref[0])
    key = rotate(head_norm(k_ref[...])[0] * gk_ref[...], cosine, sine).astype(low_type)
    value = v_ref[...].astype(low_type)
    for member in range(q_ref.shape[1] // head):
        cols = pl.ds(member * head, head)
        query = rotate(head_norm(q_ref[:, cols])[0] * gq_ref[...], cosine, sine).astype(low_type)
        probs = softmax_rows(query, key, allowed, scaling).astype(low_type)
        attended = jnp.dot(probs, value, preferred_element_type=wide_type)
        out_ref[:, cols] = (attended * jax.nn.sigmoid(g_ref[:, cols])).astype(low_type)


def attention_backward(
    q_ref,
    k_ref,
    v_ref,
    g_ref,
    cos_ref,
    sin_ref,
    col_ref,
    row_ref,
    gq_ref,
    gk_ref,
    grad_ref,
    dq_ref,
    dk_ref,
    dv_ref,
    dg_ref,
    gain_ref,
):
    head = k_ref.shape[1]
    scaling = head ** (-0.5)
    cosine, sine = cos_ref[...], sin_ref[...]
    allowed = allowed_pairs(col_ref[0], row_ref[0])
    key_normal, key_inverse = head_norm(k_ref[...])
    key = rotate(key_normal * gk_ref[...], cosine, sine).astype(low_type)
    value = v_ref[...].astype(low_type)
    grad_value = jnp.zeros(value.shape, wide_type)
    grad_key = jnp.zeros(value.shape, wide_type)
    query_gain = jnp.zeros((1, head), wide_type)
    for member in range(q_ref.shape[1] // head):
        cols = pl.ds(member * head, head)
        query_normal, query_inverse = head_norm(q_ref[:, cols])
        query = rotate(query_normal * gq_ref[...], cosine, sine).astype(low_type)
        probs = softmax_rows(query, key, allowed, scaling)
        probs_low = probs.astype(low_type)
        attended = jnp.dot(probs_low, value, preferred_element_type=wide_type)
        gate = jax.nn.sigmoid(g_ref[:, cols])
        grad_gated = grad_ref[:, cols].astype(wide_type)
        grad_attended = (grad_gated * gate).astype(low_type)
        dg_ref[:, cols] = (grad_gated * attended * gate * (1.0 - gate)).astype(low_type)
        grad_value = grad_value + dot_tn(probs_low, grad_attended)
        grad_probs = dot_nt(grad_attended, value)
        mixed = jnp.sum(probs * grad_probs, axis=-1, keepdims=True)
        grad_scores = (probs * (grad_probs - mixed) * scaling).astype(low_type)
        grad_query = rotate_back(
            jnp.dot(grad_scores, key, preferred_element_type=wide_type), cosine, sine
        )
        grad_key = grad_key + dot_tn(grad_scores, query)
        query_gain = query_gain + jnp.sum(grad_query * query_normal, axis=0, keepdims=True)
        dq_ref[:, cols] = norm_rows_back(
            query_normal, query_inverse, gq_ref[...], grad_query
        ).astype(low_type)
    grad_key = rotate_back(grad_key, cosine, sine)
    dk_ref[...] = norm_rows_back(key_normal, key_inverse, gk_ref[...], grad_key).astype(low_type)
    dv_ref[...] = grad_value.astype(low_type)
    gain_ref[0, 0, 0:1] = query_gain
    gain_ref[0, 0, 1:2] = jnp.sum(grad_key * key_normal, axis=0, keepdims=True)


def attention_specs(length, head, group, kv_heads):
    wide = group * head
    specs = [
        pl.BlockSpec((length, wide), lambda s, k: (s, k)),
        pl.BlockSpec((length, head), lambda s, k: (s, kv_heads * group + k)),
        pl.BlockSpec((length, head), lambda s, k: (s, kv_heads * (group + 1) + k)),
        pl.BlockSpec((length, wide), lambda s, k: (s, kv_heads * (group + 2) // group + k)),
        pl.BlockSpec((length, head), lambda s, k: (s, 0)),
        pl.BlockSpec((length, head), lambda s, k: (s, 0)),
        pl.BlockSpec((1, length, 1), lambda s, k: (s, 0, 0)),
        pl.BlockSpec((1, 1, length), lambda s, k: (s, 0, 0)),
        pl.BlockSpec((1, head), lambda s, k: (0, 0)),
        pl.BlockSpec((1, head), lambda s, k: (0, 0)),
    ]
    return specs, specs[0], pl.BlockSpec((length, head), lambda s, k: (s, k))


def attention_calls(seqs, length, head, group, kv_heads, interpret=False):
    specs, wide_spec, head_spec = attention_specs(length, head, group, kv_heads)
    tokens = seqs * length
    wide = jax.ShapeDtypeStruct((tokens, kv_heads * group * head), low_type)
    narrow = jax.ShapeDtypeStruct((tokens, kv_heads * head), low_type)
    gains = jax.ShapeDtypeStruct((seqs, kv_heads, 2, head), wide_type)
    forward = pl.pallas_call(
        attention_forward,
        grid=(seqs, kv_heads),
        in_specs=specs,
        out_specs=wide_spec,
        out_shape=wide,
        interpret=interpret,
    )
    backward = pl.pallas_call(
        attention_backward,
        grid=(seqs, kv_heads),
        in_specs=specs + [wide_spec],
        out_specs=[
            wide_spec,
            head_spec,
            head_spec,
            wide_spec,
            pl.BlockSpec((1, 1, 2, head), lambda s, k: (s, k, 0, 0)),
        ],
        out_shape=[wide, narrow, narrow, wide, gains],
        interpret=interpret,
    )
    return forward, backward


def transpose_block(in_ref, out_ref):
    out_ref[...] = in_ref[...].T


def turned(grad):
    rows, cols = grad.shape
    step = min(cols, 256)
    return pl.pallas_call(
        transpose_block,
        grid=(cols // step,),
        in_specs=[pl.BlockSpec((rows, step), lambda i: (0, i))],
        out_specs=pl.BlockSpec((step, rows), lambda i: (i, 0)),
        out_shape=jax.ShapeDtypeStruct((cols, rows), grad.dtype),
    )(grad)


def matmul(left, right):
    return jnp.dot(left, right, preferred_element_type=wide_type)


def matmul_nt(left, right):
    return jnp.einsum("tf,df->td", left, right, preferred_element_type=wide_type)


def matmul_tn(left, right):
    return jnp.einsum("td,tf->df", left, right, preferred_element_type=wide_type)


def swap_pairs(size, bit):
    return [(place, place ^ bit) for place in range(size)]


def after(value, *earlier):
    if isinstance(value, tuple):
        return tuple(after(part, *earlier) for part in value)
    return lax.optimization_barrier((value,) + earlier)[0] if earlier else value


def halves(rows_of, side, extent, axis):
    half = extent // 2
    return (
        lax.dynamic_slice_in_dim(rows_of, (1 - side) * half, half, axis),
        lax.dynamic_slice_in_dim(rows_of, side * half, half, axis),
    )


def tensor_scatter(make, operands, rank, size, fill=()):
    rows = operands[0].shape[0]
    split = [halves(operand, rank % 2, rows, 0) for operand in operands]
    sent = make(*[pair[0] for pair in split]).astype(low_type)
    received = lax.ppermute(sent, "tensor", swap_pairs(size, 1))
    kept = make(*[pair[1] for pair in split])
    kept = kept + after(received, kept).astype(wide_type)
    rows, bit = rows // 2, 2
    while bit < size:
        sent, kept = halves(kept, (rank // bit) % 2, rows, 0)
        received = lax.ppermute(sent.astype(low_type), "tensor", swap_pairs(size, bit))
        kept = kept + after(received, *fill).astype(wide_type)
        rows, bit = rows // 2, bit * 2
    return kept


def share_start(rank, size, rows):
    start, bit = 0, 1
    while bit < size:
        rows = rows // 2
        start = start + ((rank // bit) % 2) * rows
        bit = bit * 2
    return start


def tensor_gather(share, rank, size, fill=()):
    bit = size // 2
    while bit >= 1:
        received = lax.ppermute(share, "tensor", swap_pairs(size, bit))
        received = after(received, *fill) if bit > 1 else received
        low_side = (rank // bit) % 2 == 0
        share = jnp.concatenate(
            [jnp.where(low_side, share, received), jnp.where(low_side, received, share)], axis=0
        )
        bit = bit // 2
    return share


def outer_route(step, inner, outer):
    return [
        (z * inner + x, ((z + step) % outer) * inner + x)
        for z in range(outer)
        for x in range(inner)
    ]


def line_send(shard, inner, outer):
    arrived = [
        lax.ppermute(shard, "dp", outer_route(step, inner, outer))
        for step in range(1, outer)
    ]
    return arrived, lax.ppermute(shard, "dp", swap_pairs(inner * outer, 1))


def pair_send(arrived, inner, outer):
    return [lax.ppermute(part, "dp", swap_pairs(inner * outer, 1)) for part in arrived]


def line_join(shard, arrived, rank, inner, outer):
    place = rank // inner
    line = lax.dynamic_update_slice_in_dim(
        jnp.zeros((outer,) + shard.shape, shard.dtype), shard[None], place, 0
    )
    for step in range(1, outer):
        line = lax.dynamic_update_slice_in_dim(
            line, arrived[step - 1][None], lax.rem(place + outer - step, outer), 0
        )
    return line


def in_order(shard, arrived, partner, passed, rank, inner, outer):
    line = line_join(shard, arrived, rank, inner, outer)
    other = line_join(partner, passed, rank, inner, outer)
    side = rank % inner
    return jnp.where(side == 0, line, other), jnp.where(side == 0, other, line)


def join_rows(pair):
    outer, rows, cols = pair[0].shape
    return jnp.stack(pair, axis=1).reshape(outer * len(pair) * rows, cols)


def join_columns(pair):
    return jnp.concatenate([part[z] for z in range(pair[0].shape[0]) for part in pair], axis=1)


def scatter_send(grad, rank, inner, outer):
    rows, cols = grad.shape[0] // (inner * outer), grad.shape[1]
    blocks = grad.reshape(outer, inner, rows, cols)
    place, side = rank // inner, rank % inner
    received = []
    for step in list(range(1, outer)) + [0]:
        sent = lax.dynamic_slice(
            blocks, (lax.rem(place + step, outer), 1 - side, 0, 0), (1, 1, rows, cols)
        ).reshape(rows, cols)
        received.append(lax.ppermute(sent, "dp", swap_pairs(inner * outer, 1)))
    return blocks, tuple(received)


def scatter_line(blocks, received, rank, inner, outer):
    place, side = rank // inner, rank % inner
    rows, cols = blocks.shape[2:]

    def block(step, theirs):
        mine = lax.dynamic_slice(
            blocks, (lax.rem(place + step, outer), side, 0, 0), (1, 1, rows, cols)
        ).reshape(rows, cols)
        return mine.astype(wide_type) + theirs.astype(wide_type)

    sent = [
        block(step, received[step - 1]).astype(low_type) for step in range(1, outer)
    ]
    arrived = tuple(
        lax.ppermute(part, "dp", outer_route(step + 1, inner, outer))
        for step, part in enumerate(sent)
    )
    return block(0, received[-1]), arrived, sent[-1]


def scatter_sum(total, arrived, *earlier):
    if earlier:
        arrived = lax.optimization_barrier(tuple(arrived) + earlier)[: len(arrived)]
    for part in arrived:
        total = total + part.astype(wide_type)
    return total


def layer(
    layer_input,
    segments,
    query_weight,
    key_matrix,
    value_matrix,
    gate_weight,
    out_weight,
    ffn_gate_weight,
    ffn_up_weight,
    ffn_down_weight,
    attn_gain,
    ffn_gain,
    query_gain,
    key_norm_gain,
    cotangent,
):
    tensor_rank, tensor_size = lax.axis_index("tensor"), lax.axis_size("tensor")
    data_rank, data_size = lax.axis_index("dp"), lax.axis_size("dp")
    inner = 2
    outer = data_size // inner
    seqs, token_length, width = layer_input.shape
    tokens = seqs * token_length
    head_size = query_gain.shape[0]
    cols_q, cols_k, cols_v = query_weight.shape[1], key_matrix.shape[1], value_matrix.shape[1]
    heads_q, heads_kv = cols_q // head_size, cols_k // head_size
    group_width = heads_q // heads_kv

    ring = (data_rank, inner, outer)
    sizes = (inner, outer)
    shard_in = jnp.concatenate([query_weight, key_matrix, value_matrix, gate_weight], axis=1)
    z_in, w_in = line_send(shard_in, *sizes)
    z_o, w_o = line_send(out_weight, *sizes)
    z_gf, w_gf = line_send(ffn_gate_weight, *sizes)
    z_up, w_up = line_send(ffn_up_weight, *sizes)
    z_dn, w_dn = line_send(ffn_down_weight, *sizes)

    flat_input = layer_input.reshape(tokens, width)
    grad_low = cotangent.reshape(tokens, width)
    first_row = share_start(tensor_rank, tensor_size, tokens)
    share_rows = tokens // tensor_size
    share_input = lax.dynamic_slice_in_dim(flat_input, first_row, share_rows, 0).astype(wide_type)
    share_cotangent = lax.dynamic_slice_in_dim(grad_low, first_row, share_rows, 0).astype(
        wide_type
    )

    cosine_table, sine_table = jax.vmap(lambda row: tables(row, head_size))(segments)
    first_normed = (norm_fwd(flat_input.astype(wide_type))[0] * attn_gain).astype(low_type)
    x_in = pair_send(z_in, *sizes)
    x_o = pair_send(z_o, *sizes)
    full_in = join_rows(in_order(shard_in, z_in, w_in, x_in, *ring))
    projected = matmul(first_normed, full_in)
    x_gf = pair_send(after(tuple(z_gf), projected), *sizes)
    attend, attend_back = attention_calls(seqs, token_length, head_size, group_width, heads_kv)
    attend_args = (
        projected,
        projected,
        projected,
        projected,
        cosine_table.reshape(tokens, head_size),
        sine_table.reshape(tokens, head_size),
        segments[:, :, None],
        segments[:, None, :],
        query_gain[None],
        key_norm_gain[None],
    )
    gated = attend(*attend_args)
    full_o = join_columns(
        in_order(
            out_weight, after(tuple(z_o), projected), w_o, after(tuple(x_o), projected), *ring
        )
    )
    x_up = pair_send(after(tuple(z_up), gated), *sizes)
    branch_one = tensor_scatter(
        lambda rows: matmul(rows, full_o), (gated,), tensor_rank, tensor_size
    )
    middle = share_input + branch_one
    normal_two, inv_two = norm_fwd(middle)
    second_normed = tensor_gather(
        (normal_two * ffn_gain).astype(low_type), tensor_rank, tensor_size
    )
    x_dn = pair_send(after(tuple(z_dn), second_normed), *sizes)
    full_gf = join_rows(in_order(ffn_gate_weight, z_gf, w_gf, after(tuple(x_gf), second_normed), *ring))
    ffn_gate = matmul(second_normed, full_gf)
    full_up = join_rows(in_order(ffn_up_weight, z_up, w_up, after(tuple(x_up), ffn_gate), *ring))
    ffn_up = matmul(second_normed, full_up)
    sig_gate = jax.nn.sigmoid(ffn_gate)
    active = ffn_gate * sig_gate
    hidden = (active * ffn_up).astype(low_type)
    weight_dn = matmul_tn(grad_low, hidden).astype(low_type)
    blocks_dn, pair_dn = scatter_send(weight_dn, *ring)
    full_dn = join_columns(
        in_order(ffn_down_weight, z_dn, w_dn, after(tuple(x_dn), weight_dn), *ring)
    )
    grad_hidden = matmul_nt(grad_low, full_dn)
    grad_ffn_gate = (grad_hidden * ffn_up * sig_gate * (1.0 + ffn_gate * (1.0 - sig_gate))).astype(
        low_type
    )
    grad_ffn_up = (grad_hidden * active).astype(low_type)
    weight_gf = matmul_tn(second_normed, grad_ffn_gate).astype(low_type)
    weight_up = matmul_tn(second_normed, grad_ffn_up).astype(low_type)
    blocks_gf, pair_gf = scatter_send(weight_gf, *ring)
    blocks_up, pair_up = scatter_send(weight_up, *ring)
    grad_second = tensor_scatter(
        lambda gate_rows, up_rows: matmul_nt(gate_rows, full_gf) + matmul_nt(up_rows, full_up),
        (grad_ffn_gate, grad_ffn_up),
        tensor_rank,
        tensor_size,
        (weight_gf,),
    )
    back_two, grad_ffn_gain = norm_back(normal_two, inv_two, ffn_gain, grad_second)
    grad_middle = share_cotangent + back_two
    share_low = grad_middle.astype(low_type)
    mine_dn, line_sum_dn, _ = scatter_line(blocks_dn, after(pair_dn, share_low), *ring)
    middle_low = tensor_gather(share_low, tensor_rank, tensor_size, (weight_up, mine_dn))

    grad_gated = matmul_nt(middle_low, full_o).astype(low_type)
    weight_o = matmul_tn(middle_low, gated).astype(low_type)
    blocks_o, pair_o = scatter_send(weight_o, *ring)
    grad_query, grad_key, grad_value, grad_gate_proj, head_gains = attend_back(
        *attend_args, grad_gated
    )
    head_gains = jnp.sum(head_gains, axis=(0, 1))
    grad_qk = jnp.concatenate([grad_query, grad_key], axis=1)
    grad_vg = jnp.concatenate([grad_value, grad_gate_proj], axis=1)
    mine_gf, line_sum_gf, _ = scatter_line(blocks_gf, after(pair_gf, grad_query), *ring)
    weight_vg = matmul_tn(first_normed, grad_vg).astype(low_type)
    weight_qk = matmul_tn(first_normed, grad_qk).astype(low_type)
    blocks_vg, pair_vg = scatter_send(weight_vg, *ring)
    blocks_qk, pair_qk = scatter_send(weight_qk, *ring)
    grad_first = tensor_scatter(
        lambda qk_rows, vg_rows: matmul_nt(qk_rows, full_in[:, : cols_q + cols_k])
        + matmul_nt(vg_rows, full_in[:, cols_q + cols_k :]),
        (grad_qk, grad_vg),
        tensor_rank,
        tensor_size,
        (weight_vg, weight_qk),
    )
    branch_two = tensor_scatter(
        lambda rows: matmul(rows, full_dn),
        (after(hidden, weight_vg, weight_qk),),
        tensor_rank,
        tensor_size,
    )
    result = tensor_gather((middle + branch_two).astype(low_type), tensor_rank, tensor_size)
    mine_up, line_sum_up, sent_up = scatter_line(blocks_up, after(pair_up, grad_first), *ring)
    mine_o, line_sum_o, sent_o = scatter_line(blocks_o, after(pair_o, sent_up), *ring)
    mine_vg, line_sum_vg, sent_vg = scatter_line(blocks_vg, after(pair_vg, sent_o), *ring)
    mine_qk, line_sum_qk, _ = scatter_line(blocks_qk, after(pair_qk, sent_vg), *ring)
    grad_dn = turned(scatter_sum(mine_dn, line_sum_dn, mine_up))
    grad_gf = scatter_sum(mine_gf, line_sum_gf, mine_up)
    grad_up = scatter_sum(mine_up, line_sum_up, mine_vg)
    grad_o = turned(scatter_sum(mine_o, line_sum_o, mine_qk))
    grads_vg = scatter_sum(mine_vg, line_sum_vg, mine_qk)
    normal_one, inv_one = norm_fwd(share_input)
    back_one, grad_attn_gain = norm_back(normal_one, inv_one, attn_gain, grad_first)
    grad_input = tensor_gather(
        (grad_middle + back_one).astype(low_type), tensor_rank, tensor_size
    ).astype(wide_type)

    grads_qk = scatter_sum(
        mine_qk, line_sum_qk, grad_input, result, grad_dn, grad_gf, grad_up, grad_o, grads_vg
    )

    gains = jnp.concatenate([grad_attn_gain, grad_ffn_gain, head_gains[0], head_gains[1]])
    for axis_name, size in (("tensor", tensor_size), ("dp", data_size)):
        bit = 1
        while bit < size:
            received = lax.ppermute(gains, axis_name, swap_pairs(size, bit))
            if axis_name == "dp" and bit > 1:
                received = after(received, grad_dn, grad_gf, grad_up, grad_o, grads_vg)
            gains = gains + received
            bit = bit * 2
    return (
        result.reshape(seqs, token_length, width),
        grad_input.reshape(seqs, token_length, width),
        grads_qk[:, :cols_q],
        grads_qk[:, cols_q:],
        grads_vg[:, :cols_v],
        grads_vg[:, cols_v:],
        grad_o,
        grad_gf,
        grad_up,
        grad_dn,
        gains[:width],
        gains[width : 2 * width],
        gains[2 * width : 2 * width + head_size],
        gains[2 * width + head_size :],
    )


def solution(mesh):
    return jax.shard_map(
        layer,
        mesh=mesh,
        in_specs=(
            P("dp", None, None),
            P("dp", None),
            P("dp", "tensor"),
            P("dp", "tensor"),
            P("dp", "tensor"),
            P("dp", "tensor"),
            P("tensor", "dp"),
            P("dp", "tensor"),
            P("dp", "tensor"),
            P("tensor", "dp"),
            P(),
            P(),
            P(),
            P(),
            P("dp", None, None),
        ),
        out_specs=(
            P("dp", None, None),
            P("dp", None, None),
            P("dp", "tensor"),
            P("dp", "tensor"),
            P("dp", "tensor"),
            P("dp", "tensor"),
            P("tensor", "dp"),
            P("dp", "tensor"),
            P("dp", "tensor"),
            P("tensor", "dp"),
            P(),
            P(),
            P(),
            P(),
        ),
        check_vma=False,
    )
```

```python
import math

import jax
import jax.numpy as jnp
from jax import lax
from jax.experimental import pallas as pl
from jax.experimental.pallas import tpu as pltpu
from jax.sharding import PartitionSpec as P


epsilon = 1e-06
low_type = jnp.bfloat16
wide_type = jnp.float32


def norm_fwd(vector_in):
    scale_inv = lax.rsqrt(jnp.mean(vector_in * vector_in, axis=-1, keepdims=True) + epsilon)
    return (vector_in * scale_inv, scale_inv)


def norm_back(normal, scale_inv, gain_vec, grad_in_rows):
    scaled = grad_in_rows * gain_vec
    grad_rows = scale_inv * (scaled - normal * jnp.mean(scaled * normal, axis=-1, keepdims=True))
    return (grad_rows, jnp.sum(grad_in_rows * normal, axis=0))


def tables(segment_row, head_size):
    token_length = segment_row.shape[0]
    places = jnp.arange(token_length, dtype=jnp.int32)
    changed = jnp.concatenate(
        [jnp.ones((1,), dtype=jnp.bool_), segment_row[1:] != segment_row[:-1]]
    )
    starts = lax.cummax(jnp.where(changed, places, jnp.zeros_like(places)), axis=0)
    position = (places - starts).astype(jnp.float32)
    frequency = jnp.exp(
        jnp.arange(head_size // 2, dtype=jnp.float32) * (-2.0 * math.log(1000000.0) / head_size)
    )
    angles = position[:, None] * frequency[None, :]
    sine = jnp.sin(angles)
    return (
        jnp.concatenate([jnp.cos(angles), jnp.cos(angles)], axis=-1),
        jnp.concatenate([-sine, sine], axis=-1),
    )


def head_norm(projected):
    inverse = lax.rsqrt(jnp.mean(projected * projected, axis=-1, keepdims=True) + epsilon)
    return projected * inverse, inverse


def rotate(rows, cosine, signed_sine):
    return rows * cosine + pltpu.roll(rows, rows.shape[-1] // 2, 1) * signed_sine


def rotate_back(grad, cosine, signed_sine):
    return grad * cosine + pltpu.roll(grad * signed_sine, grad.shape[-1] // 2, 1)


def norm_rows_back(normal, inverse, gain, grad):
    scaled = grad * gain
    return inverse * (scaled - normal * jnp.mean(scaled * normal, axis=-1, keepdims=True))


def dot_nt(left, right):
    return lax.dot_general(left, right, (((1,), (1,)), ((), ())), preferred_element_type=wide_type)


def dot_tn(left, right):
    return lax.dot_general(left, right, (((0,), (0,)), ((), ())), preferred_element_type=wide_type)


def allowed_pairs(seg_col, seg_row):
    shape = (seg_col.shape[0], seg_row.shape[1])
    later = lax.broadcasted_iota(jnp.int32, shape, 0) >= lax.broadcasted_iota(jnp.int32, shape, 1)
    return (seg_col == seg_row) & later


def softmax_rows(query, key, allowed, scaling):
    scores = jnp.where(allowed, dot_nt(query, key) * scaling, -1000000000.0)
    exponent = jnp.exp(scores - jnp.max(scores, axis=-1, keepdims=True))
    return exponent / jnp.sum(exponent, axis=-1, keepdims=True)


def attention_forward(
    q_ref, k_ref, v_ref, g_ref, cos_ref, sin_ref, col_ref, row_ref, gq_ref, gk_ref, out_ref
):
    head = k_ref.shape[1]
    scaling = head ** (-0.5)
    cosine, sine = cos_ref[...], sin_ref[...]
    allowed = allowed_pairs(col_ref[0], row_ref[0])
    key = rotate(head_norm(k_ref[...])[0] * gk_ref[...], cosine, sine).astype(low_type)
    value = v_ref[...].astype(low_type)
    for member in range(q_ref.shape[1] // head):
        cols = pl.ds(member * head, head)
        query = rotate(head_norm(q_ref[:, cols])[0] * gq_ref[...], cosine, sine).astype(low_type)
        probs = softmax_rows(query, key, allowed, scaling).astype(low_type)
        attended = jnp.dot(probs, value, preferred_element_type=wide_type)
        out_ref[:, cols] = (attended * jax.nn.sigmoid(g_ref[:, cols])).astype(low_type)


def attention_backward(
    q_ref,
    k_ref,
    v_ref,
    g_ref,
    cos_ref,
    sin_ref,
    col_ref,
    row_ref,
    gq_ref,
    gk_ref,
    grad_ref,
    dq_ref,
    dk_ref,
    dv_ref,
    dg_ref,
    gain_ref,
):
    head = k_ref.shape[1]
    scaling = head ** (-0.5)
    cosine, sine = cos_ref[...], sin_ref[...]
    allowed = allowed_pairs(col_ref[0], row_ref[0])
    key_normal, key_inverse = head_norm(k_ref[...])
    key = rotate(key_normal * gk_ref[...], cosine, sine).astype(low_type)
    value = v_ref[...].astype(low_type)
    grad_value = jnp.zeros(value.shape, wide_type)
    grad_key = jnp.zeros(value.shape, wide_type)
    query_gain = jnp.zeros((1, head), wide_type)
    for member in range(q_ref.shape[1] // head):
        cols = pl.ds(member * head, head)
        query_normal, query_inverse = head_norm(q_ref[:, cols])
        query = rotate(query_normal * gq_ref[...], cosine, sine).astype(low_type)
        probs = softmax_rows(query, key, allowed, scaling)
        probs_low = probs.astype(low_type)
        attended = jnp.dot(probs_low, value, preferred_element_type=wide_type)
        gate = jax.nn.sigmoid(g_ref[:, cols])
        grad_gated = grad_ref[:, cols].astype(wide_type)
        grad_attended = (grad_gated * gate).astype(low_type)
        dg_ref[:, cols] = (grad_gated * attended * gate * (1.0 - gate)).astype(low_type)
        grad_value = grad_value + dot_tn(probs_low, grad_attended)
        grad_probs = dot_nt(grad_attended, value)
        mixed = jnp.sum(probs * grad_probs, axis=-1, keepdims=True)
        grad_scores = (probs * (grad_probs - mixed) * scaling).astype(low_type)
        grad_query = rotate_back(
            jnp.dot(grad_scores, key, preferred_element_type=wide_type), cosine, sine
        )
        grad_key = grad_key + dot_tn(grad_scores, query)
        query_gain = query_gain + jnp.sum(grad_query * query_normal, axis=0, keepdims=True)
        dq_ref[:, cols] = norm_rows_back(
            query_normal, query_inverse, gq_ref[...], grad_query
        ).astype(low_type)
    grad_key = rotate_back(grad_key, cosine, sine)
    dk_ref[...] = norm_rows_back(key_normal, key_inverse, gk_ref[...], grad_key).astype(low_type)
    dv_ref[...] = grad_value.astype(low_type)
    gain_ref[0, 0, 0:1] = query_gain
    gain_ref[0, 0, 1:2] = jnp.sum(grad_key * key_normal, axis=0, keepdims=True)


def attention_specs(length, head, group, kv_heads):
    wide = group * head
    specs = [
        pl.BlockSpec((length, wide), lambda s, k: (s, k)),
        pl.BlockSpec((length, head), lambda s, k: (s, kv_heads * group + k)),
        pl.BlockSpec((length, head), lambda s, k: (s, kv_heads * (group + 1) + k)),
        pl.BlockSpec((length, wide), lambda s, k: (s, kv_heads * (group + 2) // group + k)),
        pl.BlockSpec((length, head), lambda s, k: (s, 0)),
        pl.BlockSpec((length, head), lambda s, k: (s, 0)),
        pl.BlockSpec((1, length, 1), lambda s, k: (s, 0, 0)),
        pl.BlockSpec((1, 1, length), lambda s, k: (s, 0, 0)),
        pl.BlockSpec((1, head), lambda s, k: (0, 0)),
        pl.BlockSpec((1, head), lambda s, k: (0, 0)),
    ]
    return specs, specs[0], pl.BlockSpec((length, head), lambda s, k: (s, k))


def attention_calls(seqs, length, head, group, kv_heads, interpret=False):
    specs, wide_spec, head_spec = attention_specs(length, head, group, kv_heads)
    tokens = seqs * length
    wide = jax.ShapeDtypeStruct((tokens, kv_heads * group * head), low_type)
    narrow = jax.ShapeDtypeStruct((tokens, kv_heads * head), low_type)
    gains = jax.ShapeDtypeStruct((seqs, kv_heads, 2, head), wide_type)
    forward = pl.pallas_call(
        attention_forward,
        grid=(seqs, kv_heads),
        in_specs=specs,
        out_specs=wide_spec,
        out_shape=wide,
        interpret=interpret,
    )
    backward = pl.pallas_call(
        attention_backward,
        grid=(seqs, kv_heads),
        in_specs=specs + [wide_spec],
        out_specs=[
            wide_spec,
            head_spec,
            head_spec,
            wide_spec,
            pl.BlockSpec((1, 1, 2, head), lambda s, k: (s, k, 0, 0)),
        ],
        out_shape=[wide, narrow, narrow, wide, gains],
        interpret=interpret,
    )
    return forward, backward


def transpose_block(in_ref, out_ref):
    out_ref[...] = in_ref[...].T


def turned(grad):
    rows, cols = grad.shape
    step = min(cols, 256)
    return pl.pallas_call(
        transpose_block,
        grid=(cols // step,),
        in_specs=[pl.BlockSpec((rows, step), lambda i: (0, i))],
        out_specs=pl.BlockSpec((step, rows), lambda i: (i, 0)),
        out_shape=jax.ShapeDtypeStruct((cols, rows), grad.dtype),
    )(grad)


def matmul(left, right):
    return jnp.dot(left, right, preferred_element_type=wide_type)


def matmul_nt(left, right):
    return jnp.einsum("tf,df->td", left, right, preferred_element_type=wide_type)


def matmul_tn(left, right):
    return jnp.einsum("td,tf->df", left, right, preferred_element_type=wide_type)


def swap_pairs(size, bit):
    return [(place, place ^ bit) for place in range(size)]


def after(value, *earlier):
    if isinstance(value, tuple):
        return tuple(after(part, *earlier) for part in value)
    return lax.optimization_barrier((value,) + earlier)[0] if earlier else value


def halves(rows_of, side, extent, axis):
    half = extent // 2
    return (
        lax.dynamic_slice_in_dim(rows_of, (1 - side) * half, half, axis),
        lax.dynamic_slice_in_dim(rows_of, side * half, half, axis),
    )


def tensor_scatter(make, operands, rank, size, fill=()):
    rows = operands[0].shape[0]
    split = [halves(operand, rank % 2, rows, 0) for operand in operands]
    sent = make(*[pair[0] for pair in split]).astype(low_type)
    received = lax.ppermute(sent, "tensor", swap_pairs(size, 1))
    kept = make(*[pair[1] for pair in split])
    kept = kept + after(received, kept).astype(wide_type)
    rows, bit = rows // 2, 2
    while bit < size:
        sent, kept = halves(kept, (rank // bit) % 2, rows, 0)
        received = lax.ppermute(sent.astype(low_type), "tensor", swap_pairs(size, bit))
        kept = kept + after(received, *fill).astype(wide_type)
        rows, bit = rows // 2, bit * 2
    return kept


def share_start(rank, size, rows):
    start, bit = 0, 1
    while bit < size:
        rows = rows // 2
        start = start + ((rank // bit) % 2) * rows
        bit = bit * 2
    return start


def tensor_gather(share, rank, size, fill=()):
    bit = size // 2
    while bit >= 1:
        received = lax.ppermute(share, "tensor", swap_pairs(size, bit))
        received = after(received, *fill) if bit > 1 else received
        low_side = (rank // bit) % 2 == 0
        share = jnp.concatenate(
            [jnp.where(low_side, share, received), jnp.where(low_side, received, share)], axis=0
        )
        bit = bit // 2
    return share


def outer_route(step, inner, outer):
    return [
        (z * inner + x, ((z + step) % outer) * inner + x)
        for z in range(outer)
        for x in range(inner)
    ]


def line_send(shard, inner, outer):
    arrived = [
        lax.ppermute(shard, "dp", outer_route(step, inner, outer))
        for step in range(1, outer)
    ]
    return arrived, lax.ppermute(shard, "dp", swap_pairs(inner * outer, 1))


def pair_send(arrived, inner, outer):
    return [lax.ppermute(part, "dp", swap_pairs(inner * outer, 1)) for part in arrived]


def line_join(shard, arrived, rank, inner, outer):
    place = rank // inner
    line = lax.dynamic_update_slice_in_dim(
        jnp.zeros((outer,) + shard.shape, shard.dtype), shard[None], place, 0
    )
    for step in range(1, outer):
        line = lax.dynamic_update_slice_in_dim(
            line, arrived[step - 1][None], lax.rem(place + outer - step, outer), 0
        )
    return line


def in_order(shard, arrived, partner, passed, rank, inner, outer):
    line = line_join(shard, arrived, rank, inner, outer)
    other = line_join(partner, passed, rank, inner, outer)
    side = rank % inner
    return jnp.where(side == 0, line, other), jnp.where(side == 0, other, line)


def join_rows(pair):
    outer, rows, cols = pair[0].shape
    return jnp.stack(pair, axis=1).reshape(outer * len(pair) * rows, cols)


def join_columns(pair):
    return jnp.concatenate([part[z] for z in range(pair[0].shape[0]) for part in pair], axis=1)


def scatter_send(grad, rank, inner, outer):
    rows, cols = grad.shape[0] // (inner * outer), grad.shape[1]
    blocks = grad.reshape(outer, inner, rows, cols)
    place, side = rank // inner, rank % inner
    received = []
    for step in list(range(1, outer)) + [0]:
        sent = lax.dynamic_slice(
            blocks, (lax.rem(place + step, outer), 1 - side, 0, 0), (1, 1, rows, cols)
        ).reshape(rows, cols)
        received.append(lax.ppermute(sent, "dp", swap_pairs(inner * outer, 1)))
    return blocks, tuple(received)


def scatter_line(blocks, received, rank, inner, outer):
    place, side = rank // inner, rank % inner
    rows, cols = blocks.shape[2:]

    def block(step, theirs):
        mine = lax.dynamic_slice(
            blocks, (lax.rem(place + step, outer), side, 0, 0), (1, 1, rows, cols)
        ).reshape(rows, cols)
        return mine.astype(wide_type) + theirs.astype(wide_type)

    sent = [
        block(step, received[step - 1]).astype(low_type) for step in range(1, outer)
    ]
    arrived = tuple(
        lax.ppermute(part, "dp", outer_route(step + 1, inner, outer))
        for step, part in enumerate(sent)
    )
    return block(0, received[-1]), arrived, sent[-1]


def scatter_sum(total, arrived, *earlier):
    if earlier:
        arrived = lax.optimization_barrier(tuple(arrived) + earlier)[: len(arrived)]
    for part in arrived:
        total = total + part.astype(wide_type)
    return total


def layer(
    layer_input,
    segments,
    query_weight,
    key_matrix,
    value_matrix,
    gate_weight,
    out_weight,
    ffn_gate_weight,
    ffn_up_weight,
    ffn_down_weight,
    attn_gain,
    ffn_gain,
    query_gain,
    key_norm_gain,
    cotangent,
):
    tensor_rank, tensor_size = lax.axis_index("tensor"), lax.axis_size("tensor")
    data_rank, data_size = lax.axis_index("dp"), lax.axis_size("dp")
    inner = 2
    outer = data_size // inner
    seqs, token_length, width = layer_input.shape
    tokens = seqs * token_length
    head_size = query_gain.shape[0]
    cols_q, cols_k, cols_v = query_weight.shape[1], key_matrix.shape[1], value_matrix.shape[1]
    heads_q, heads_kv = cols_q // head_size, cols_k // head_size
    group_width = heads_q // heads_kv

    ring = (data_rank, inner, outer)
    sizes = (inner, outer)
    shard_in = jnp.concatenate([query_weight, key_matrix, value_matrix, gate_weight], axis=1)
    z_in, w_in = line_send(shard_in, *sizes)
    z_o, w_o = line_send(out_weight, *sizes)
    z_gf, w_gf = line_send(ffn_gate_weight, *sizes)
    z_up, w_up = line_send(ffn_up_weight, *sizes)
    z_dn, w_dn = line_send(ffn_down_weight, *sizes)

    flat_input = layer_input.reshape(tokens, width)
    grad_low = cotangent.reshape(tokens, width)
    first_row = share_start(tensor_rank, tensor_size, tokens)
    share_rows = tokens // tensor_size
    share_input = lax.dynamic_slice_in_dim(flat_input, first_row, share_rows, 0).astype(wide_type)
    share_cotangent = lax.dynamic_slice_in_dim(grad_low, first_row, share_rows, 0).astype(
        wide_type
    )

    cosine_table, sine_table = jax.vmap(lambda row: tables(row, head_size))(segments)
    first_normed = (norm_fwd(flat_input.astype(wide_type))[0] * attn_gain).astype(low_type)
    x_in = pair_send(z_in, *sizes)
    x_o = pair_send(z_o, *sizes)
    full_in = join_rows(in_order(shard_in, z_in, w_in, x_in, *ring))
    projected = matmul(first_normed, full_in)
    x_gf = pair_send(after(tuple(z_gf), projected), *sizes)
    attend, attend_back = attention_calls(seqs, token_length, head_size, group_width, heads_kv)
    attend_args = (
        projected,
        projected,
        projected,
        projected,
        cosine_table.reshape(tokens, head_size),
        sine_table.reshape(tokens, head_size),
        segments[:, :, None],
        segments[:, None, :],
        query_gain[None],
        key_norm_gain[None],
    )
    gated = attend(*attend_args)
    full_o = join_columns(
        in_order(
            out_weight, after(tuple(z_o), projected), w_o, after(tuple(x_o), projected), *ring
        )
    )
    x_up = pair_send(after(tuple(z_up), gated), *sizes)
    branch_one = tensor_scatter(
        lambda rows: matmul(rows, full_o), (gated,), tensor_rank, tensor_size
    )
    middle = share_input + branch_one
    normal_two, inv_two = norm_fwd(middle)
    second_normed = tensor_gather(
        (normal_two * ffn_gain).astype(low_type), tensor_rank, tensor_size
    )
    full_gf = join_rows(in_order(ffn_gate_weight, z_gf, w_gf, after(tuple(x_gf), second_normed), *ring))
    ffn_gate = matmul(second_normed, full_gf)
    full_up = join_rows(in_order(ffn_up_weight, z_up, w_up, after(tuple(x_up), ffn_gate), *ring))
    ffn_up = matmul(second_normed, full_up)
    sig_gate = jax.nn.sigmoid(ffn_gate)
    active = ffn_gate * sig_gate
    hidden = (active * ffn_up).astype(low_type)
    x_dn = pair_send(after(tuple(z_dn), hidden), *sizes)
    weight_dn = matmul_tn(grad_low, hidden).astype(low_type)
    blocks_dn, pair_dn = scatter_send(weight_dn, *ring)
    full_dn = join_columns(
        in_order(ffn_down_weight, z_dn, w_dn, after(tuple(x_dn), weight_dn), *ring)
    )
    grad_hidden = matmul_nt(grad_low, full_dn)
    grad_ffn_gate = (grad_hidden * ffn_up * sig_gate * (1.0 + ffn_gate * (1.0 - sig_gate))).astype(
        low_type
    )
    grad_ffn_up = (grad_hidden * active).astype(low_type)
    weight_gf = matmul_tn(second_normed, grad_ffn_gate).astype(low_type)
    weight_up = matmul_tn(second_normed, grad_ffn_up).astype(low_type)
    blocks_gf, pair_gf = scatter_send(weight_gf, *ring)
    blocks_up, pair_up = scatter_send(weight_up, *ring)
    mine_dn, line_sum_dn, sent_dn = scatter_line(blocks_dn, after(pair_dn, weight_gf), *ring)
    grad_second = tensor_scatter(
        lambda gate_rows, up_rows: matmul_nt(gate_rows, full_gf) + matmul_nt(up_rows, full_up),
        (grad_ffn_gate, grad_ffn_up),
        tensor_rank,
        tensor_size,
        (weight_gf, sent_dn),
    )
    back_two, grad_ffn_gain = norm_back(normal_two, inv_two, ffn_gain, grad_second)
    grad_middle = share_cotangent + back_two
    share_low = grad_middle.astype(low_type)
    middle_low = tensor_gather(share_low, tensor_rank, tensor_size, (weight_up,))

    grad_gated = matmul_nt(middle_low, full_o).astype(low_type)
    weight_o = matmul_tn(middle_low, gated).astype(low_type)
    blocks_o, pair_o = scatter_send(weight_o, *ring)
    grad_query, grad_key, grad_value, grad_gate_proj, head_gains = attend_back(
        *attend_args, grad_gated
    )
    head_gains = jnp.sum(head_gains, axis=(0, 1))
    grad_qk = jnp.concatenate([grad_query, grad_key], axis=1)
    grad_vg = jnp.concatenate([grad_value, grad_gate_proj], axis=1)
    mine_gf, line_sum_gf, _ = scatter_line(blocks_gf, after(pair_gf, grad_query), *ring)
    weight_vg = matmul_tn(first_normed, grad_vg).astype(low_type)
    weight_qk = matmul_tn(first_normed, grad_qk).astype(low_type)
    blocks_vg, pair_vg = scatter_send(weight_vg, *ring)
    blocks_qk, pair_qk = scatter_send(weight_qk, *ring)
    mine_up, line_sum_up, sent_up = scatter_line(blocks_up, pair_up, *ring)
    grad_first = tensor_scatter(
        lambda qk_rows, vg_rows: matmul_nt(qk_rows, full_in[:, : cols_q + cols_k])
        + matmul_nt(vg_rows, full_in[:, cols_q + cols_k :]),
        (grad_qk, grad_vg),
        tensor_rank,
        tensor_size,
        (weight_vg, weight_qk, sent_up),
    )
    branch_two = tensor_scatter(
        lambda rows: matmul(rows, full_dn),
        (after(hidden, weight_vg, weight_qk),),
        tensor_rank,
        tensor_size,
        (sent_up,),
    )
    result = tensor_gather((middle + branch_two).astype(low_type), tensor_rank, tensor_size)
    mine_o, line_sum_o, _ = scatter_line(blocks_o, pair_o, *ring)
    mine_vg, line_sum_vg, _ = scatter_line(blocks_vg, pair_vg, *ring)
    mine_qk, line_sum_qk, _ = scatter_line(blocks_qk, pair_qk, *ring)
    grad_dn = turned(scatter_sum(mine_dn, line_sum_dn, mine_up))
    grad_gf = scatter_sum(mine_gf, line_sum_gf, mine_up)
    grad_up = scatter_sum(mine_up, line_sum_up, mine_vg)
    grad_o = turned(scatter_sum(mine_o, line_sum_o, mine_qk))
    grads_vg = scatter_sum(mine_vg, line_sum_vg, mine_qk)
    normal_one, inv_one = norm_fwd(share_input)
    back_one, grad_attn_gain = norm_back(normal_one, inv_one, attn_gain, grad_first)
    grad_input = tensor_gather(
        (grad_middle + back_one).astype(low_type), tensor_rank, tensor_size
    ).astype(wide_type)

    grads_qk = scatter_sum(
        mine_qk, line_sum_qk, grad_input, result, grad_dn, grad_gf, grad_up, grad_o, grads_vg
    )

    gains = jnp.concatenate([grad_attn_gain, grad_ffn_gain, head_gains[0], head_gains[1]])
    for axis_name, size in (("tensor", tensor_size), ("dp", data_size)):
        bit = 1
        while bit < size:
            received = lax.ppermute(gains, axis_name, swap_pairs(size, bit))
            if axis_name == "dp" and bit > 1:
                received = after(received, grad_dn, grad_gf, grad_up, grad_o, grads_vg)
            gains = gains + received
            bit = bit * 2
    return (
        result.reshape(seqs, token_length, width),
        grad_input.reshape(seqs, token_length, width),
        grads_qk[:, :cols_q],
        grads_qk[:, cols_q:],
        grads_vg[:, :cols_v],
        grads_vg[:, cols_v:],
        grad_o,
        grad_gf,
        grad_up,
        grad_dn,
        gains[:width],
        gains[width : 2 * width],
        gains[2 * width : 2 * width + head_size],
        gains[2 * width + head_size :],
    )


def solution(mesh):
    return jax.shard_map(
        layer,
        mesh=mesh,
        in_specs=(
            P("dp", None, None),
            P("dp", None),
            P("dp", "tensor"),
            P("dp", "tensor"),
            P("dp", "tensor"),
            P("dp", "tensor"),
            P("tensor", "dp"),
            P("dp", "tensor"),
            P("dp", "tensor"),
            P("tensor", "dp"),
            P(),
            P(),
            P(),
            P(),
            P("dp", None, None),
        ),
        out_specs=(
            P("dp", None, None),
            P("dp", None, None),
            P("dp", "tensor"),
            P("dp", "tensor"),
            P("dp", "tensor"),
            P("dp", "tensor"),
            P("tensor", "dp"),
            P("dp", "tensor"),
            P("dp", "tensor"),
            P("tensor", "dp"),
            P(),
            P(),
            P(),
            P(),
        ),
        check_vma=False,
    )
```

```python
import math

import jax
import jax.numpy as jnp
from jax import lax
from jax.experimental import pallas as pl
from jax.experimental.pallas import tpu as pltpu
from jax.sharding import PartitionSpec as P


epsilon = 1e-06
low_type = jnp.bfloat16
wide_type = jnp.float32


def norm_fwd(vector_in):
    scale_inv = lax.rsqrt(jnp.mean(vector_in * vector_in, axis=-1, keepdims=True) + epsilon)
    return (vector_in * scale_inv, scale_inv)


def norm_back(normal, scale_inv, gain_vec, grad_in_rows):
    scaled = grad_in_rows * gain_vec
    grad_rows = scale_inv * (scaled - normal * jnp.mean(scaled * normal, axis=-1, keepdims=True))
    return (grad_rows, jnp.sum(grad_in_rows * normal, axis=0))


def tables(segment_row, head_size):
    token_length = segment_row.shape[0]
    places = jnp.arange(token_length, dtype=jnp.int32)
    changed = jnp.concatenate(
        [jnp.ones((1,), dtype=jnp.bool_), segment_row[1:] != segment_row[:-1]]
    )
    starts = lax.cummax(jnp.where(changed, places, jnp.zeros_like(places)), axis=0)
    position = (places - starts).astype(jnp.float32)
    frequency = jnp.exp(
        jnp.arange(head_size // 2, dtype=jnp.float32) * (-2.0 * math.log(1000000.0) / head_size)
    )
    angles = position[:, None] * frequency[None, :]
    sine = jnp.sin(angles)
    return (
        jnp.concatenate([jnp.cos(angles), jnp.cos(angles)], axis=-1),
        jnp.concatenate([-sine, sine], axis=-1),
    )


def head_norm(projected):
    inverse = lax.rsqrt(jnp.mean(projected * projected, axis=-1, keepdims=True) + epsilon)
    return projected * inverse, inverse


def rotate(rows, cosine, signed_sine):
    return rows * cosine + pltpu.roll(rows, rows.shape[-1] // 2, 1) * signed_sine


def rotate_back(grad, cosine, signed_sine):
    return grad * cosine + pltpu.roll(grad * signed_sine, grad.shape[-1] // 2, 1)


def norm_rows_back(normal, inverse, gain, grad):
    scaled = grad * gain
    return inverse * (scaled - normal * jnp.mean(scaled * normal, axis=-1, keepdims=True))


def dot_nt(left, right):
    return lax.dot_general(left, right, (((1,), (1,)), ((), ())), preferred_element_type=wide_type)


def dot_tn(left, right):
    return lax.dot_general(left, right, (((0,), (0,)), ((), ())), preferred_element_type=wide_type)


def allowed_pairs(seg_col, seg_row):
    shape = (seg_col.shape[0], seg_row.shape[1])
    later = lax.broadcasted_iota(jnp.int32, shape, 0) >= lax.broadcasted_iota(jnp.int32, shape, 1)
    return (seg_col == seg_row) & later


def softmax_rows(query, key, allowed, scaling):
    scores = jnp.where(allowed, dot_nt(query, key) * scaling, -1000000000.0)
    exponent = jnp.exp(scores - jnp.max(scores, axis=-1, keepdims=True))
    return exponent / jnp.sum(exponent, axis=-1, keepdims=True)


def attention_forward(
    q_ref, k_ref, v_ref, g_ref, cos_ref, sin_ref, col_ref, row_ref, gq_ref, gk_ref, out_ref
):
    head = k_ref.shape[1]
    scaling = head ** (-0.5)
    cosine, sine = cos_ref[...], sin_ref[...]
    allowed = allowed_pairs(col_ref[0], row_ref[0])
    key = rotate(head_norm(k_ref[...])[0] * gk_ref[...], cosine, sine).astype(low_type)
    value = v_ref[...].astype(low_type)
    for member in range(q_ref.shape[1] // head):
        cols = pl.ds(member * head, head)
        query = rotate(head_norm(q_ref[:, cols])[0] * gq_ref[...], cosine, sine).astype(low_type)
        probs = softmax_rows(query, key, allowed, scaling).astype(low_type)
        attended = jnp.dot(probs, value, preferred_element_type=wide_type)
        out_ref[:, cols] = (attended * jax.nn.sigmoid(g_ref[:, cols])).astype(low_type)


def attention_backward(
    q_ref,
    k_ref,
    v_ref,
    g_ref,
    cos_ref,
    sin_ref,
    col_ref,
    row_ref,
    gq_ref,
    gk_ref,
    grad_ref,
    dq_ref,
    dk_ref,
    dv_ref,
    dg_ref,
    gain_ref,
):
    head = k_ref.shape[1]
    scaling = head ** (-0.5)
    cosine, sine = cos_ref[...], sin_ref[...]
    allowed = allowed_pairs(col_ref[0], row_ref[0])
    key_normal, key_inverse = head_norm(k_ref[...])
    key = rotate(key_normal * gk_ref[...], cosine, sine).astype(low_type)
    value = v_ref[...].astype(low_type)
    grad_value = jnp.zeros(value.shape, wide_type)
    grad_key = jnp.zeros(value.shape, wide_type)
    query_gain = jnp.zeros((1, head), wide_type)
    for member in range(q_ref.shape[1] // head):
        cols = pl.ds(member * head, head)
        query_normal, query_inverse = head_norm(q_ref[:, cols])
        query = rotate(query_normal * gq_ref[...], cosine, sine).astype(low_type)
        probs = softmax_rows(query, key, allowed, scaling)
        probs_low = probs.astype(low_type)
        attended = jnp.dot(probs_low, value, preferred_element_type=wide_type)
        gate = jax.nn.sigmoid(g_ref[:, cols])
        grad_gated = grad_ref[:, cols].astype(wide_type)
        grad_attended = (grad_gated * gate).astype(low_type)
        dg_ref[:, cols] = (grad_gated * attended * gate * (1.0 - gate)).astype(low_type)
        grad_value = grad_value + dot_tn(probs_low, grad_attended)
        grad_probs = dot_nt(grad_attended, value)
        mixed = jnp.sum(probs * grad_probs, axis=-1, keepdims=True)
        grad_scores = (probs * (grad_probs - mixed) * scaling).astype(low_type)
        grad_query = rotate_back(
            jnp.dot(grad_scores, key, preferred_element_type=wide_type), cosine, sine
        )
        grad_key = grad_key + dot_tn(grad_scores, query)
        query_gain = query_gain + jnp.sum(grad_query * query_normal, axis=0, keepdims=True)
        dq_ref[:, cols] = norm_rows_back(
            query_normal, query_inverse, gq_ref[...], grad_query
        ).astype(low_type)
    grad_key = rotate_back(grad_key, cosine, sine)
    dk_ref[...] = norm_rows_back(key_normal, key_inverse, gk_ref[...], grad_key).astype(low_type)
    dv_ref[...] = grad_value.astype(low_type)
    gain_ref[0, 0, 0:1] = query_gain
    gain_ref[0, 0, 1:2] = jnp.sum(grad_key * key_normal, axis=0, keepdims=True)


def attention_specs(length, head, group, kv_heads):
    wide = group * head
    specs = [
        pl.BlockSpec((length, wide), lambda s, k: (s, k)),
        pl.BlockSpec((length, head), lambda s, k: (s, kv_heads * group + k)),
        pl.BlockSpec((length, head), lambda s, k: (s, kv_heads * (group + 1) + k)),
        pl.BlockSpec((length, wide), lambda s, k: (s, kv_heads * (group + 2) // group + k)),
        pl.BlockSpec((length, head), lambda s, k: (s, 0)),
        pl.BlockSpec((length, head), lambda s, k: (s, 0)),
        pl.BlockSpec((1, length, 1), lambda s, k: (s, 0, 0)),
        pl.BlockSpec((1, 1, length), lambda s, k: (s, 0, 0)),
        pl.BlockSpec((1, head), lambda s, k: (0, 0)),
        pl.BlockSpec((1, head), lambda s, k: (0, 0)),
    ]
    return specs, specs[0], pl.BlockSpec((length, head), lambda s, k: (s, k))


def attention_calls(seqs, length, head, group, kv_heads, interpret=False):
    specs, wide_spec, head_spec = attention_specs(length, head, group, kv_heads)
    tokens = seqs * length
    wide = jax.ShapeDtypeStruct((tokens, kv_heads * group * head), low_type)
    narrow = jax.ShapeDtypeStruct((tokens, kv_heads * head), low_type)
    gains = jax.ShapeDtypeStruct((seqs, kv_heads, 2, head), wide_type)
    forward = pl.pallas_call(
        attention_forward,
        grid=(seqs, kv_heads),
        in_specs=specs,
        out_specs=wide_spec,
        out_shape=wide,
        interpret=interpret,
    )
    backward = pl.pallas_call(
        attention_backward,
        grid=(seqs, kv_heads),
        in_specs=specs + [wide_spec],
        out_specs=[
            wide_spec,
            head_spec,
            head_spec,
            wide_spec,
            pl.BlockSpec((1, 1, 2, head), lambda s, k: (s, k, 0, 0)),
        ],
        out_shape=[wide, narrow, narrow, wide, gains],
        interpret=interpret,
    )
    return forward, backward


def transpose_block(in_ref, out_ref):
    out_ref[...] = in_ref[...].T


def turned(grad):
    rows, cols = grad.shape
    step = min(cols, 256)
    return pl.pallas_call(
        transpose_block,
        grid=(cols // step,),
        in_specs=[pl.BlockSpec((rows, step), lambda i: (0, i))],
        out_specs=pl.BlockSpec((step, rows), lambda i: (i, 0)),
        out_shape=jax.ShapeDtypeStruct((cols, rows), grad.dtype),
    )(grad)


def matmul(left, right):
    return jnp.dot(left, right, preferred_element_type=wide_type)


def matmul_nt(left, right):
    return jnp.einsum("tf,df->td", left, right, preferred_element_type=wide_type)


def matmul_tn(left, right):
    return jnp.einsum("td,tf->df", left, right, preferred_element_type=wide_type)


def swap_pairs(size, bit):
    return [(place, place ^ bit) for place in range(size)]


def after(value, *earlier):
    if isinstance(value, tuple):
        return tuple(after(part, *earlier) for part in value)
    return lax.optimization_barrier((value,) + earlier)[0] if earlier else value


def halves(rows_of, side, extent, axis):
    half = extent // 2
    return (
        lax.dynamic_slice_in_dim(rows_of, (1 - side) * half, half, axis),
        lax.dynamic_slice_in_dim(rows_of, side * half, half, axis),
    )


def tensor_scatter(make, operands, rank, size, fill=()):
    rows = operands[0].shape[0]
    split = [halves(operand, rank % 2, rows, 0) for operand in operands]
    sent = make(*[pair[0] for pair in split]).astype(low_type)
    received = lax.ppermute(sent, "tensor", swap_pairs(size, 1))
    kept = make(*[pair[1] for pair in split])
    kept = kept + after(received, kept).astype(wide_type)
    rows, bit = rows // 2, 2
    while bit < size:
        sent, kept = halves(kept, (rank // bit) % 2, rows, 0)
        received = lax.ppermute(sent.astype(low_type), "tensor", swap_pairs(size, bit))
        kept = kept + after(received, *fill).astype(wide_type)
        rows, bit = rows // 2, bit * 2
    return kept


def share_start(rank, size, rows):
    start, bit = 0, 1
    while bit < size:
        rows = rows // 2
        start = start + ((rank // bit) % 2) * rows
        bit = bit * 2
    return start


def tensor_gather(share, rank, size, fill=()):
    bit = size // 2
    while bit >= 1:
        received = lax.ppermute(share, "tensor", swap_pairs(size, bit))
        received = after(received, *fill) if bit > 1 else received
        low_side = (rank // bit) % 2 == 0
        share = jnp.concatenate(
            [jnp.where(low_side, share, received), jnp.where(low_side, received, share)], axis=0
        )
        bit = bit // 2
    return share


def outer_route(step, inner, outer):
    return [
        (z * inner + x, ((z + step) % outer) * inner + x)
        for z in range(outer)
        for x in range(inner)
    ]


def moves(pairs, inner):
    return [(a * inner + x, b * inner + x) for a, b in pairs for x in range(inner)]


def line_send(shard, inner, outer):
    if outer != 4:
        return tuple(
            lax.ppermute(shard, "dp", outer_route(step, inner, outer))
            for step in range(1, outer)
        )
    routes = (((0, 1), (1, 2), (2, 3)), ((1, 0), (2, 1), (3, 2)), ((0, 2), (3, 1)))
    return tuple(lax.ppermute(shard, "dp", moves(route, inner)) for route in routes)


def own_send(shard, inner, outer):
    return lax.ppermute(shard, "dp", swap_pairs(inner * outer, 1))


def line_relay(arrived, inner, outer):
    if outer != 4:
        return ()
    below, above, beyond = arrived
    return (
        lax.ppermute(below, "dp", moves(((2, 3),), inner)),
        lax.ppermute(above, "dp", moves(((1, 0),), inner)),
        lax.ppermute(beyond, "dp", moves(((2, 3), (1, 0)), inner)),
    )


def line_parts(arrived, relayed, rank, inner, outer):
    place = rank // inner
    if outer != 4:
        return arrived, [lax.rem(place + outer - step, outer) for step in range(1, outer)]
    below, above, beyond = arrived
    first, last = place == 0, place == 3
    ends = first | last
    parts = (
        jnp.where(first, above, below),
        jnp.where(first, relayed[1], jnp.where(last, relayed[0], above)),
        jnp.where(ends, relayed[2], beyond),
    )
    places = [
        jnp.where(first, 1, place - 1),
        jnp.where(first, 2, jnp.where(last, 1, place + 1)),
        jnp.where(place < 2, 3, 0),
    ]
    return parts, places


def pair_send(parts, inner, outer):
    return tuple(lax.ppermute(part, "dp", swap_pairs(inner * outer, 1)) for part in parts)


def line_join(shard, parts, places, rank, inner, outer):
    line = lax.dynamic_update_slice_in_dim(
        jnp.zeros((outer,) + shard.shape, shard.dtype), shard[None], rank // inner, 0
    )
    for part, which in zip(parts, places):
        line = lax.dynamic_update_slice_in_dim(line, part[None], which, 0)
    return line


def in_order(shard, parts, places, partner, passed, rank, inner, outer):
    line = line_join(shard, parts, places, rank, inner, outer)
    other = line_join(partner, passed, places, rank, inner, outer)
    side = rank % inner
    return jnp.where(side == 0, line, other), jnp.where(side == 0, other, line)


def join_rows(pair):
    outer, rows, cols = pair[0].shape
    return jnp.stack(pair, axis=1).reshape(outer * len(pair) * rows, cols)


def join_columns(pair):
    return jnp.concatenate([part[z] for z in range(pair[0].shape[0]) for part in pair], axis=1)


def scatter_send(grad, rank, inner, outer):
    rows, cols = grad.shape[0] // (inner * outer), grad.shape[1]
    blocks = grad.reshape(outer, inner, rows, cols)
    place, side = rank // inner, rank % inner
    received = []
    for step in list(range(1, outer)) + [0]:
        sent = lax.dynamic_slice(
            blocks, (lax.rem(place + step, outer), 1 - side, 0, 0), (1, 1, rows, cols)
        ).reshape(rows, cols)
        received.append(lax.ppermute(sent, "dp", swap_pairs(inner * outer, 1)))
    return blocks, tuple(received)


def scatter_line(blocks, received, rank, inner, outer):
    place, side = rank // inner, rank % inner
    rows, cols = blocks.shape[2:]

    def block(step, theirs):
        mine = lax.dynamic_slice(
            blocks, (lax.rem(place + step, outer), side, 0, 0), (1, 1, rows, cols)
        ).reshape(rows, cols)
        return mine.astype(wide_type) + theirs.astype(wide_type)

    sent = [
        block(step, received[step - 1]).astype(low_type) for step in range(1, outer)
    ]
    arrived = tuple(
        lax.ppermute(part, "dp", outer_route(step + 1, inner, outer))
        for step, part in enumerate(sent)
    )
    return block(0, received[-1]), arrived, sent[-1]


def scatter_sum(total, arrived, *earlier):
    if earlier:
        arrived = lax.optimization_barrier(tuple(arrived) + earlier)[: len(arrived)]
    for part in arrived:
        total = total + part.astype(wide_type)
    return total


def layer(
    layer_input,
    segments,
    query_weight,
    key_matrix,
    value_matrix,
    gate_weight,
    out_weight,
    ffn_gate_weight,
    ffn_up_weight,
    ffn_down_weight,
    attn_gain,
    ffn_gain,
    query_gain,
    key_norm_gain,
    cotangent,
):
    tensor_rank, tensor_size = lax.axis_index("tensor"), lax.axis_size("tensor")
    data_rank, data_size = lax.axis_index("dp"), lax.axis_size("dp")
    inner = 2
    outer = data_size // inner
    seqs, token_length, width = layer_input.shape
    tokens = seqs * token_length
    head_size = query_gain.shape[0]
    cols_q, cols_k, cols_v = query_weight.shape[1], key_matrix.shape[1], value_matrix.shape[1]
    heads_q, heads_kv = cols_q // head_size, cols_k // head_size
    group_width = heads_q // heads_kv

    ring = (data_rank, inner, outer)
    sizes = (inner, outer)
    shard_in = jnp.concatenate([query_weight, key_matrix, value_matrix, gate_weight], axis=1)
    held = (
        ("in", shard_in),
        ("o", out_weight),
        ("gf", ffn_gate_weight),
        ("up", ffn_up_weight),
        ("dn", ffn_down_weight),
    )
    near = {name: line_send(shard, *sizes) for name, shard in held}
    owned = {name: own_send(shard, *sizes) for name, shard in held}

    def pass_on(name, *earlier):
        arrived = after(near[name], *earlier)
        parts, places = line_parts(arrived, line_relay(arrived, *sizes), *ring)
        return parts, places, pair_send(parts, *sizes)

    def ordered(name, shard, gathered, *earlier):
        parts, places, passed = gathered
        return in_order(
            shard, after(parts, *earlier), places, owned[name], after(passed, *earlier), *ring
        )

    flat_input = layer_input.reshape(tokens, width)
    grad_low = cotangent.reshape(tokens, width)
    first_row = share_start(tensor_rank, tensor_size, tokens)
    share_rows = tokens // tensor_size
    share_input = lax.dynamic_slice_in_dim(flat_input, first_row, share_rows, 0).astype(wide_type)
    share_cotangent = lax.dynamic_slice_in_dim(grad_low, first_row, share_rows, 0).astype(
        wide_type
    )

    cosine_table, sine_table = jax.vmap(lambda row: tables(row, head_size))(segments)
    first_normed = (norm_fwd(flat_input.astype(wide_type))[0] * attn_gain).astype(low_type)
    got_in = pass_on("in")
    got_o = pass_on("o")
    got_gf = pass_on("gf")
    full_in = join_rows(ordered("in", shard_in, got_in))
    projected = matmul(first_normed, full_in)
    attend, attend_back = attention_calls(seqs, token_length, head_size, group_width, heads_kv)
    attend_args = (
        projected,
        projected,
        projected,
        projected,
        cosine_table.reshape(tokens, head_size),
        sine_table.reshape(tokens, head_size),
        segments[:, :, None],
        segments[:, None, :],
        query_gain[None],
        key_norm_gain[None],
    )
    gated = attend(*attend_args)
    full_o = join_columns(ordered("o", out_weight, got_o, projected))
    got_up = pass_on("up", gated)
    branch_one = tensor_scatter(
        lambda rows: matmul(rows, full_o), (gated,), tensor_rank, tensor_size
    )
    middle = share_input + branch_one
    normal_two, inv_two = norm_fwd(middle)
    second_share = (normal_two * ffn_gain).astype(low_type)
    second_normed = tensor_gather(second_share, tensor_rank, tensor_size)
    got_dn = pass_on("dn", second_share)
    full_gf = join_rows(ordered("gf", ffn_gate_weight, got_gf, second_normed))
    ffn_gate = matmul(second_normed, full_gf)
    full_up = join_rows(ordered("up", ffn_up_weight, got_up, ffn_gate))
    ffn_up = matmul(second_normed, full_up)
    sig_gate = jax.nn.sigmoid(ffn_gate)
    active = ffn_gate * sig_gate
    hidden = (active * ffn_up).astype(low_type)
    weight_dn = matmul_tn(grad_low, hidden).astype(low_type)
    blocks_dn, pair_dn = scatter_send(weight_dn, *ring)
    full_dn = join_columns(ordered("dn", ffn_down_weight, got_dn, weight_dn))
    grad_hidden = matmul_nt(grad_low, full_dn)
    grad_ffn_gate = (grad_hidden * ffn_up * sig_gate * (1.0 + ffn_gate * (1.0 - sig_gate))).astype(
        low_type
    )
    grad_ffn_up = (grad_hidden * active).astype(low_type)
    weight_gf = matmul_tn(second_normed, grad_ffn_gate).astype(low_type)
    weight_up = matmul_tn(second_normed, grad_ffn_up).astype(low_type)
    blocks_gf, pair_gf = scatter_send(weight_gf, *ring)
    blocks_up, pair_up = scatter_send(weight_up, *ring)
    mine_dn, line_sum_dn, sent_dn = scatter_line(blocks_dn, after(pair_dn, weight_gf), *ring)
    grad_second = tensor_scatter(
        lambda gate_rows, up_rows: matmul_nt(gate_rows, full_gf) + matmul_nt(up_rows, full_up),
        (grad_ffn_gate, grad_ffn_up),
        tensor_rank,
        tensor_size,
        (weight_gf, sent_dn),
    )
    back_two, grad_ffn_gain = norm_back(normal_two, inv_two, ffn_gain, grad_second)
    grad_middle = share_cotangent + back_two
    share_low = grad_middle.astype(low_type)
    middle_low = tensor_gather(share_low, tensor_rank, tensor_size, (weight_up,))

    grad_gated = matmul_nt(middle_low, full_o).astype(low_type)
    weight_o = matmul_tn(middle_low, gated).astype(low_type)
    blocks_o, pair_o = scatter_send(weight_o, *ring)
    grad_query, grad_key, grad_value, grad_gate_proj, head_gains = attend_back(
        *attend_args, grad_gated
    )
    head_gains = jnp.sum(head_gains, axis=(0, 1))
    grad_qk = jnp.concatenate([grad_query, grad_key], axis=1)
    grad_vg = jnp.concatenate([grad_value, grad_gate_proj], axis=1)
    mine_gf, line_sum_gf, _ = scatter_line(blocks_gf, after(pair_gf, grad_query), *ring)
    weight_vg = matmul_tn(first_normed, grad_vg).astype(low_type)
    weight_qk = matmul_tn(first_normed, grad_qk).astype(low_type)
    blocks_vg, pair_vg = scatter_send(weight_vg, *ring)
    blocks_qk, pair_qk = scatter_send(weight_qk, *ring)
    mine_up, line_sum_up, sent_up = scatter_line(blocks_up, pair_up, *ring)
    grad_first = tensor_scatter(
        lambda qk_rows, vg_rows: matmul_nt(qk_rows, full_in[:, : cols_q + cols_k])
        + matmul_nt(vg_rows, full_in[:, cols_q + cols_k :]),
        (grad_qk, grad_vg),
        tensor_rank,
        tensor_size,
        (weight_vg, weight_qk, sent_up),
    )
    branch_two = tensor_scatter(
        lambda rows: matmul(rows, full_dn),
        (after(hidden, weight_vg, weight_qk),),
        tensor_rank,
        tensor_size,
        (sent_up,),
    )
    result = tensor_gather((middle + branch_two).astype(low_type), tensor_rank, tensor_size)
    mine_o, line_sum_o, _ = scatter_line(blocks_o, pair_o, *ring)
    mine_vg, line_sum_vg, _ = scatter_line(blocks_vg, pair_vg, *ring)
    mine_qk, line_sum_qk, _ = scatter_line(blocks_qk, pair_qk, *ring)
    grad_dn = turned(scatter_sum(mine_dn, line_sum_dn, mine_up))
    grad_gf = scatter_sum(mine_gf, line_sum_gf, mine_up)
    grad_up = scatter_sum(mine_up, line_sum_up, mine_vg)
    grad_o = turned(scatter_sum(mine_o, line_sum_o, mine_qk))
    grads_vg = scatter_sum(mine_vg, line_sum_vg, mine_qk)
    normal_one, inv_one = norm_fwd(share_input)
    back_one, grad_attn_gain = norm_back(normal_one, inv_one, attn_gain, grad_first)
    grad_input = tensor_gather(
        (grad_middle + back_one).astype(low_type), tensor_rank, tensor_size
    ).astype(wide_type)

    grads_qk = scatter_sum(
        mine_qk, line_sum_qk, grad_input, result, grad_dn, grad_gf, grad_up, grad_o, grads_vg
    )

    gains = jnp.concatenate([grad_attn_gain, grad_ffn_gain, head_gains[0], head_gains[1]])
    for axis_name, size in (("tensor", tensor_size), ("dp", data_size)):
        bit = 1
        while bit < size:
            received = lax.ppermute(gains, axis_name, swap_pairs(size, bit))
            if axis_name == "dp" and bit > 1:
                received = after(received, grad_dn, grad_gf, grad_up, grad_o, grads_vg)
            gains = gains + received
            bit = bit * 2
    return (
        result.reshape(seqs, token_length, width),
        grad_input.reshape(seqs, token_length, width),
        grads_qk[:, :cols_q],
        grads_qk[:, cols_q:],
        grads_vg[:, :cols_v],
        grads_vg[:, cols_v:],
        grad_o,
        grad_gf,
        grad_up,
        grad_dn,
        gains[:width],
        gains[width : 2 * width],
        gains[2 * width : 2 * width + head_size],
        gains[2 * width + head_size :],
    )


def solution(mesh):
    return jax.shard_map(
        layer,
        mesh=mesh,
        in_specs=(
            P("dp", None, None),
            P("dp", None),
            P("dp", "tensor"),
            P("dp", "tensor"),
            P("dp", "tensor"),
            P("dp", "tensor"),
            P("tensor", "dp"),
            P("dp", "tensor"),
            P("dp", "tensor"),
            P("tensor", "dp"),
            P(),
            P(),
            P(),
            P(),
            P("dp", None, None),
        ),
        out_specs=(
            P("dp", None, None),
            P("dp", None, None),
            P("dp", "tensor"),
            P("dp", "tensor"),
            P("dp", "tensor"),
            P("dp", "tensor"),
            P("tensor", "dp"),
            P("dp", "tensor"),
            P("dp", "tensor"),
            P("tensor", "dp"),
            P(),
            P(),
            P(),
            P(),
        ),
        check_vma=False,
    )
```
